128 devices in a mesh: side: 2 (over y_lo), grp: 8 (over y_hi, z), cuts: 8 (over x, core).
Axes of the slice: x: 4, y: 4 (y_hi: 2, y_lo: 2; y = y_hi * 2 + y_lo), z: 4, core: 2. Of those that a mesh axis runs over, the one named last changes fastest.
Arguments:
- query: bfloat16 [512, 6144], P(('side', 'grp', 'cuts')), may hold values from -21 to 21, as said below
- k_cache: bfloat16 [512, 256, 1024], P(('side', 'grp', 'cuts')), may hold values from -5 to 5
- v_cache: bfloat16 [512, 256, 1024], P(('side', 'grp', 'cuts')), may hold values from -6 to 6
- new_key: bfloat16 [512, 1024], P(('side', 'grp', 'cuts')), may hold values from -6 to 6
- new_value: bfloat16 [512, 1024], P(('side', 'grp', 'cuts')), may hold values from -6 to 6
- lengths: int32 [512], P(('side', 'grp', 'cuts')), may hold values from 2 to 256, as said below
- residual: bfloat16 [512, 6144], P(('side', 'grp', 'cuts')), may hold values from -6 to 6
- norm_gain: bfloat16 [6144], replicated, may hold values from 0.099609375 to 1.8984375
- router: bfloat16 [6144, 8], replicated, may hold values from -0.078125 to 0.078125
- routes: int32 [512, 2], P(('side', 'grp', 'cuts')), may hold values from 0 to 7, all different within a row; in each aligned block of 4 rows (0 to 3, 4 to 7, ...) at most 2 rows name the same one
- w_gate: bfloat16 [8, 6144, 8192], P('grp', None, ('side', 'cuts')), may hold values from -0.078125 to 0.078125
- w_up: bfloat16 [8, 6144, 8192], P('grp', None, ('side', 'cuts')), may hold values from -0.078125 to 0.078125
- w_down: bfloat16 [8, 8192, 6144], P('grp', ('side', 'cuts')), may hold values from -0.0625 to 0.0625
Outputs:
- layer_out: bfloat16 [512, 6144], P(('side', 'grp', 'cuts'))
The draws below stay inside these ranges and needn't reach their ends.
Inputs may be any that keep to these rules, and one draw needn't show every extreme that they name: `query`: queries are the new token's queries; in some draws a few rows have queries aligned with some cached keys. `lengths`: some row in every draw has all 256 positions live. `routes`: the two experts of a row differ. Within the rows of one device (aligned blocks of 4 rows) no expert is named more than 2 times, a bound that some block of every draw reaches.
All inputs are finite; a program needn't handle non-finite values.
Results may differ from the reference program's by a relative error of at most 0.0095.
Values may be sent and summed in bfloat16 or wider, within the bound.
A program may use at most 128 MiB of HBM per device.

```python
import math
import jax
import jax.numpy as jnp
import numpy as np
from jax import lax

Q_HEADS = 48
KV_HEADS = 8
HEAD_DIM = 128
D = 6144
FF = 8192
ROW_DEV = 4
SPAN = 256
EXPERTS = 8
MOST = 2
ROWS = 512
N_SIDE = 2
N_CUTS = 8


def draw_query(key, part):
    own = jax.random.fold_in(key, 21)
    return jnp.clip(jax.random.normal(own, (ROWS, D), jnp.float32), -4.5, 4.5).astype(jnp.bfloat16)


def draw_k_cache(key, part):
    own = jax.random.fold_in(key, 22)
    return jnp.clip(jax.random.normal(own, (ROWS, SPAN, KV_HEADS * HEAD_DIM), jnp.float32), -4.5, 4.5).astype(jnp.bfloat16)


def draw_lengths(key, part):
    lowest = max(2, SPAN // 8)
    drawn = jax.random.randint(jax.random.fold_in(key, 31), (ROWS,), lowest, SPAN + 1)
    filled = jax.random.randint(jax.random.fold_in(key, 32), (), 0, ROWS)
    return jnp.where(jnp.arange(ROWS) == filled, SPAN, drawn).astype(jnp.int32)


def level_of(rng, shape, pieces, smallest, top_value):
    factor_of, own = 1.0, jax.random.fold_in(rng, 6)
    for position, parts in pieces:
        heights = jnp.exp(jax.random.uniform(jax.random.fold_in(own, position), (parts,), jnp.float32, smallest / len(pieces), top_value / len(pieces)))
        factor_of = factor_of * jnp.repeat(heights, shape[position] // parts).reshape([-1 if axis == position else 1 for axis in range(len(shape))])
    return factor_of


def shared_out(key, own, number, rows, count, top, limit, slope):
    ranking = jax.random.permutation(key, count)
    crowded, common = load_shares(count, rows * top, limit, slope, True), load_shares(count, rows * top, limit, slope, False)
    places = jnp.arange(count)

    def named(sizes, turn):
        used = int((sizes > 0).sum())
        fixed = max(1, used // 4)
        shifted = fixed + (places - fixed + turn * (used - fixed)) % max(1, count - fixed)
        return jnp.zeros((count,), jnp.int32).at[ranking[jnp.where(places < fixed, places, shifted)]].set(jnp.asarray(sizes, jnp.int32))

    sizes = jnp.where(number % 4 == 0, named(crowded, number // 4), named(common, number - number // 4 - 1))
    mixed = jax.random.permutation(jax.random.fold_in(own, 3), count)
    source_of, taker = mixed[0:count // 2 * 2:2], mixed[1:count // 2 * 2:2]
    margin = jnp.minimum(sizes[source_of] - 1, limit - sizes[taker]) // 2
    margin = jnp.where((source_of == ranking[0]) | (taker == ranking[0]) | (sizes[taker] == 0), 0, jnp.maximum(margin, 0))
    shifted = jax.random.randint(jax.random.fold_in(own, 4), (count // 2,), 0, 1 << 20) % (margin + 1)
    sizes = sizes.at[source_of].add(-shifted).at[taker].add(shifted)
    labels = jnp.searchsorted(jnp.cumsum(sizes), jnp.arange(rows * top), side="right").astype(jnp.int32)
    listing = labels.reshape(top, rows).T
    listing = listing[jax.random.permutation(jax.random.fold_in(own, 1), rows)]
    turn = jax.random.randint(jax.random.fold_in(own, 2), (rows, 1), 0, top)
    return jnp.take_along_axis(listing, (jnp.arange(top)[None, :] + turn) % top, axis=1)


def load_shares(count, total, reach, slope, full):
    loads = [(1 << 20) // math.isqrt(rank ** slope) + 1 for rank in range(1, count + 1)]
    largest = reach if full else min(reach, max(-(-total // count), total * loads[0] // sum(loads)))
    least = 1 if total - largest >= count - 1 else 0
    given, spare = [largest] + [least] * (count - 1), total - largest - least * (count - 1)
    while spare > 0:
        movable = [i for i in range(1, count) if given[i] < largest] or [i for i in range(1, count) if given[i] < reach]
        whole, remaining = sum([loads[i] for i in movable]), spare
        for i in movable:
            more = min(reach - given[i], max(1, remaining * loads[i] // whole), spare)
            given[i] = given[i] + more
            spare = spare - more
    return np.array(given)


def normal_values(key, extent, scale, limit, split=(), kind=jnp.bfloat16):
    entries = jax.random.normal(key, extent, jnp.float32) * scale
    if len(split) > 0:
        entries = level_of(key, extent, split, -0.22, 0.18) * entries
    return jnp.clip(entries, min=-limit, max=limit).astype(kind)


def setup_inputs(seed: int = 0) -> dict:
    key_list = jax.random.split(jax.random.key(seed), 14)
    query = draw_query(jax.random.fold_in(key_list[13], 71), 0)
    k_cache = draw_k_cache(jax.random.fold_in(key_list[13], 71), 0)
    v_cache = normal_values(key_list[2], (ROWS, SPAN, KV_HEADS * HEAD_DIM), 1.0, 6.0, ((0, 128),))
    new_key = normal_values(key_list[3], (ROWS, KV_HEADS * HEAD_DIM), 1.0, 6.0, ((0, 128),))
    new_value = normal_values(key_list[4], (ROWS, KV_HEADS * HEAD_DIM), 1.0, 6.0, ((0, 128),))
    lengths = draw_lengths(jax.random.fold_in(key_list[13], 71), 0)
    residual = normal_values(key_list[6], (ROWS, D), 1.0, 6.0, ((0, 128),))
    norm_gain = jnp.clip(1.0 + 0.18 * jax.random.normal(key_list[7], (D,), jnp.float32), 0.099609375, 1.8984375).astype(jnp.bfloat16)
    router = normal_values(key_list[8], (D, EXPERTS), D ** -0.5, 0.078125)
    routes_keys = jax.random.split(jax.random.fold_in(key_list[9], 1), ROWS // ROW_DEV)
    routes_turns = jax.random.permutation(jax.random.fold_in(key_list[9], 3), ROWS // ROW_DEV)
    routes = jax.vmap(lambda own, number: shared_out(jax.random.fold_in(key_list[9], 2), own, number, ROW_DEV, EXPERTS, 2, MOST, 2))(routes_keys, routes_turns).reshape((ROWS, 2))
    w_gate = normal_values(key_list[10], (EXPERTS, D, FF), D ** -0.5, 0.078125, ((0, 8), (2, 16)))
    w_up = normal_values(key_list[11], (EXPERTS, D, FF), D ** -0.5, 0.078125, ((0, 8), (2, 16)))
    w_down = normal_values(key_list[12], (EXPERTS, FF, D), FF ** -0.5, 0.0625, ((0, 8), (1, 16)))
    return dict(query=query, k_cache=k_cache, v_cache=v_cache, new_key=new_key, new_value=new_value, lengths=lengths, residual=residual, norm_gain=norm_gain, router=router, routes=routes, w_gate=w_gate, w_up=w_up, w_down=w_down)


def attend(query, k_cache, v_cache, new_key, new_value, lengths):
    rows, span, _ = k_cache.shape
    group = Q_HEADS // KV_HEADS
    scale = 1.0 / math.sqrt(HEAD_DIM)
    queries = query.astype(jnp.float32).reshape(rows, KV_HEADS, group, HEAD_DIM)
    keys = k_cache.astype(jnp.float32).reshape(rows, span, KV_HEADS, HEAD_DIM)
    values = v_cache.astype(jnp.float32).reshape(rows, span, KV_HEADS, HEAD_DIM)
    fresh_key = new_key.astype(jnp.float32).reshape(rows, KV_HEADS, HEAD_DIM)
    fresh_value = new_value.astype(jnp.float32).reshape(rows, KV_HEADS, 1, HEAD_DIM)
    old = jnp.einsum('rkgd,rskd->rkgs', queries, keys) * scale
    own = jnp.einsum('rkgd,rkd->rkg', queries, fresh_key) * scale
    live = jnp.arange(span)[None, :] < lengths[:, None]
    old = jnp.where(live[:, None, None, :], old, -jnp.inf)
    top = jnp.maximum(lax.optimization_barrier(jnp.max(old, axis=-1)), own)
    e_old = jnp.exp(old - top[..., None])
    e_own = jnp.exp(own - top)
    total = lax.optimization_barrier(jnp.sum(e_old, axis=-1)) + e_own
    p_old = (e_old / total[..., None]).astype(jnp.bfloat16).astype(jnp.float32)
    p_own = (e_own / total).astype(jnp.bfloat16).astype(jnp.float32)
    out = jnp.einsum('rkgs,rskd->rkgd', p_old, values) + p_own[..., None] * fresh_value
    return out.reshape(rows, Q_HEADS * HEAD_DIM)

def slot_ranks(block):
    flat = block.reshape(-1)
    order = jnp.arange(flat.shape[0])
    same = (flat[:, None] == flat[None, :]) & (order[None, :] < order[:, None])
    return lax.optimization_barrier(jnp.sum(same.astype(jnp.int32), axis=1)).reshape(block.shape)

def reference(query, k_cache, v_cache, new_key, new_value, lengths, residual, norm_gain, router, routes, w_gate, w_up, w_down):
    attended = attend(query, k_cache, v_cache, new_key, new_value, lengths)
    mixed = residual.astype(jnp.float32) + attended
    power = lax.optimization_barrier(jnp.mean(mixed * mixed, axis=1, keepdims=True))
    normed = (mixed * lax.rsqrt(power + 1e-05) * norm_gain.astype(jnp.float32)).astype(jnp.bfloat16)
    logits = jnp.dot(normed, router, preferred_element_type=jnp.float32)
    picked = jnp.take_along_axis(logits, routes, axis=1)
    first = jax.nn.sigmoid(picked[:, 0] - picked[:, 1])
    second = jax.nn.sigmoid(picked[:, 1] - picked[:, 0])
    blocks_count = ROWS // ROW_DEV
    blocks = routes.reshape(blocks_count, ROW_DEV, 2)
    ranks = jax.vmap(slot_ranks)(blocks)
    normed_blocks = normed.reshape(blocks_count, ROW_DEV, D).astype(jnp.float32)
    slot_ids = jnp.arange(MOST).astype(jnp.int32)
    slices = N_SIDE * N_CUTS
    slice_width = FF // slices

    def one_expert(item):
        expert_id, gate_w, up_w, down_w = item
        match = (blocks == expert_id)[:, None] & (ranks[:, None] == slot_ids[None, :, None, None])
        pick = lax.optimization_barrier(jnp.sum(match.astype(jnp.float32), axis=-1))
        buffer = jnp.einsum('bmr,brx->bmx', pick, normed_blocks).astype(jnp.bfloat16).reshape(blocks_count * MOST, D)
        gate = jnp.dot(buffer, gate_w, preferred_element_type=jnp.float32)
        upper = jnp.dot(buffer, up_w, preferred_element_type=jnp.float32)
        act = (jax.nn.silu(gate) * upper).astype(jnp.bfloat16)
        summed = jnp.zeros((blocks_count * MOST, D), jnp.float32)
        for index in range(slices):
            low = index * slice_width
            piece = jnp.dot(act[:, low:low + slice_width], down_w[low:low + slice_width], preferred_element_type=jnp.float32)
            piece = lax.optimization_barrier(piece.astype(jnp.bfloat16))
            summed = summed + piece.astype(jnp.float32)
        return summed
    expert_ids = jnp.arange(EXPERTS).astype(jnp.int32)
    results = lax.map(one_expert, (expert_ids, w_gate, w_up, w_down))
    owner = (jnp.arange(ROWS) // ROW_DEV).astype(jnp.int32)
    slot_index = (owner[:, None] * MOST + ranks.reshape(ROWS, 2)).astype(jnp.int32)
    taken = results[routes, slot_index]
    total = mixed + first[:, None] * taken[:, 0] + second[:, None] * taken[:, 1]
    return total.astype(jnp.bfloat16)
```

```python
import math

import jax
import jax.numpy as jnp
from jax import lax
from jax.experimental import pallas as pl
from jax.experimental.pallas import tpu as pltpu
from jax.sharding import PartitionSpec as P

Q_HEADS = 48
KV_HEADS = 8
HEAD_DIM = 128
CHUNKS = 8
MESH = pl.DeviceIdType.MESH


def attend(query, k_cache, v_cache, new_key, new_value, lengths):
    rows, span, _ = k_cache.shape
    group = Q_HEADS // KV_HEADS
    scale = 1.0 / math.sqrt(HEAD_DIM)
    queries = query.reshape(rows, KV_HEADS, group, HEAD_DIM)
    keys = k_cache.reshape(rows, span, KV_HEADS, HEAD_DIM)
    values = v_cache.reshape(rows, span, KV_HEADS, HEAD_DIM)
    fresh_key = new_key.reshape(rows, KV_HEADS, HEAD_DIM)
    fresh_value = new_value.astype(jnp.float32).reshape(rows, KV_HEADS, 1, HEAD_DIM)
    old = jnp.einsum("rkgd,rskd->rkgs", queries, keys, preferred_element_type=jnp.float32) * scale
    own = (
        jnp.einsum("rkgd,rkd->rkg", queries, fresh_key, preferred_element_type=jnp.float32) * scale
    )
    live = jnp.arange(span)[None, :] < lengths[:, None]
    old = jnp.where(live[:, None, None, :], old, -jnp.inf)
    top = jnp.maximum(jnp.max(old, axis=-1), own)
    e_old = jnp.exp(old - top[..., None])
    e_own = jnp.exp(own - top)
    total = jnp.sum(e_old, axis=-1) + e_own
    p_old = (e_old / total[..., None]).astype(jnp.bfloat16)
    p_own = (e_own / total).astype(jnp.bfloat16).astype(jnp.float32)
    out = jnp.einsum("rkgs,rskd->rkgd", p_old, values, preferred_element_type=jnp.float32)
    out = out + p_own[..., None] * fresh_value
    return out.reshape(rows, Q_HEADS * HEAD_DIM)


def slot_ranks(block):
    flat = block.reshape(-1)
    order = jnp.arange(flat.shape[0])
    same = (flat[:, None] == flat[None, :]) & (order[None, :] < order[:, None])
    return jnp.sum(same.astype(jnp.int32), axis=1).reshape(block.shape)


def expert_kernel(
    slots, wg_hbm, wu_hbm, wd_hbm, ret,
    wg, wu, wd, arrived, flat, rows_in, gate, upper, act,
    own, pair_out, pair_in, raw_out, hop_in, raw_in, sum_out, sum_in, side_out, side_in,
    back_out, back_in,
    w_sem, loc_sem, go_send, go_recv, ag_send, ag_recv, rs_send, rs_recv, re_send, re_recv,
):
    n, height, width = rows_in.shape
    half = height // 2
    heads = slots.shape[1]
    part = heads // n
    most = 2
    experts = lax.axis_size("grp")
    block = experts * most
    s, g, c = lax.axis_index("side"), lax.axis_index("grp"), lax.axis_index("cuts")
    x, core = c // 2, lax.rem(c, 2)
    other = (1 - s, g, c)
    right = (s, g, lax.rem(x + 1, 4) * 2 + core)
    left = (s, g, lax.rem(x + 3, 4) * 2 + core)
    mate = (s, g, x * 2 + 1 - core)

    def peer(k):
        return lax.rem(g + k, experts)

    loads = []
    for i in range(n):
        loads.append((
            pltpu.make_async_copy(wg_hbm.at[pl.ds(i * width, width), :], wg.at[i], w_sem.at[0, i]),
            pltpu.make_async_copy(wu_hbm.at[pl.ds(i * width, width), :], wu.at[i], w_sem.at[1, i]),
        ))
    for i in range(n):
        loads.append((
            pltpu.make_async_copy(wd_hbm.at[:, pl.ds(i * width, width)], wd.at[i], w_sem.at[2, i]),
        ))
    for group in loads:
        for copy in group:
            copy.start()

    barrier = pltpu.get_barrier_semaphore()
    for k in range(1, experts):
        pl.semaphore_signal(barrier, inc=1, device_id=(s, peer(k), c), device_id_type=MESH)
    for device in (other, right, left, mate):
        pl.semaphore_signal(barrier, inc=1, device_id=device, device_id_type=MESH)
    pl.semaphore_wait(barrier, experts + 3)

    def go(k):
        return pltpu.make_async_remote_copy(
            slots.at[pl.ds(peer(k) * most, most)], arrived.at[pl.ds(g * most, most)],
            go_send.at[k], go_recv.at[k], device_id=(s, peer(k), c), device_id_type=MESH,
        )

    for k in range(1, experts):
        go(k).start()
    mine = pltpu.make_async_copy(
        slots.at[pl.ds(g * most, most)], arrived.at[pl.ds(g * most, most)], loc_sem.at[0]
    )
    mine.start()
    gate[...] = jnp.zeros_like(gate)
    upper[...] = jnp.zeros_like(upper)
    mine.wait()
    for k in range(1, experts):
        go(k).wait_recv()

    flat[...] = arrived[...].reshape(block * heads, HEAD_DIM).astype(jnp.float32)
    for h in range(heads):
        rows_in[h // part, 0:block, (h % part) * HEAD_DIM:(h % part + 1) * HEAD_DIM] = flat[
            pl.ds(h, block, stride=heads), :
        ].astype(jnp.bfloat16)

    table = (
        (0, 4, other), (0, 3, right), (0, 1, left), (4, 7, right), (4, 5, left), (3, 2, right), (5, 6, left),
    )

    def ag(i, j):
        if j == 7:
            src, dst, device = pl.ds(0, half), pl.ds(half, half), mate
        else:
            a, b, device = table[j]
            src, dst = pl.ds(a * block, block), pl.ds(b * block, block)
        return pltpu.make_async_remote_copy(
            rows_in.at[i, src, :], rows_in.at[i, dst, :], ag_send.at[i, j], ag_recv.at[i, j],
            device_id=device, device_id_type=MESH,
        )

    def first(i):
        for j in (0, 1, 2):
            ag(i, j).start()

    ahead = 3
    for i in range(ahead):
        first(i)

    def gather_step(t, carry):
        @pl.when(t + ahead < n)
        def _():
            first(t + ahead)

        @pl.when(t < n)
        def _():
            ag(t, 0).wait_recv()
            ag(t, 3).start()
            ag(t, 4).start()
            ag(t, 1).wait_recv()
            ag(t, 5).start()

        @pl.when((t >= 1) & (t < n + 1))
        def _():
            ag(t - 1, 4).wait_recv()
            ag(t - 1, 6).start()

        @pl.when((t >= 2) & (t < n + 2))
        def _():
            for j in (2, 3, 5, 6):
                ag(t - 2, j).wait_recv()
            ag(t - 2, 7).start()

        @pl.when(t >= 3)
        def _():
            i = t - 3
            ag(i, 7).wait_recv()
            pltpu.make_async_copy(wg_hbm.at[pl.ds(0, width), :], wg.at[i], w_sem.at[0, i]).wait()
            pltpu.make_async_copy(wu_hbm.at[pl.ds(0, width), :], wu.at[i], w_sem.at[1, i]).wait()
            gate[...] += jnp.dot(rows_in[i], wg[i], preferred_element_type=jnp.float32)
            upper[...] += jnp.dot(rows_in[i], wu[i], preferred_element_type=jnp.float32)

        return carry

    lax.fori_loop(0, n + 3, gather_step, 0)
    v = gate[...]
    act[...] = (v / (1.0 + jnp.exp(-v)) * upper[...]).astype(jnp.bfloat16)

    def rs(i, k):
        src, dst, device = (
            (pair_out.at[i], pair_in.at[i], mate),
            (raw_out.at[i, 0], hop_in.at[i, 0], right),
            (raw_out.at[i, 1], hop_in.at[i, 1], left),
            (raw_out.at[i, 2], raw_in.at[i, 0], right),
            (raw_out.at[i, 3], raw_in.at[i, 1], left),
            (sum_out.at[i, 0], sum_in.at[i, 0], right),
            (sum_out.at[i, 1], sum_in.at[i, 1], left),
            (side_out.at[i], side_in.at[i], other),
        )[k]
        return pltpu.make_async_remote_copy(
            src, dst, rs_send.at[i, k], rs_recv.at[i, k], device_id=device, device_id_type=MESH
        )

    def of(k):
        return pl.ds(k * block, block)

    def f32(value):
        return value.astype(jnp.float32)

    def reduce_step(t, carry):
        @pl.when(t < n)
        def _():
            pltpu.make_async_copy(wd_hbm.at[:, pl.ds(0, width)], wd.at[t], w_sem.at[2, t]).wait()
            product = jnp.dot(act[...], wd[t], preferred_element_type=jnp.float32)
            pair_out[t] = product[half:].astype(jnp.bfloat16)
            own[t] = product[:half]
            rs(t, 0).start()

        @pl.when((t >= 1) & (t < n + 1))
        def _():
            i = t - 1
            rs(i, 0).wait_recv()
            total = own[i] + f32(pair_in[i])
            for place, k in enumerate((2, 6, 5, 3)):
                raw_out[i, place] = total[k * block:(k + 1) * block].astype(jnp.bfloat16)
            own[i] = total
            for k in (1, 2, 3, 4):
                rs(i, k).start()

        @pl.when((t >= 2) & (t < n + 2))
        def _():
            i = t - 2
            rs(i, 1).wait_recv()
            sum_out[i, 0] = (own[i, of(1), :] + f32(hop_in[i, 0])).astype(jnp.bfloat16)
            rs(i, 5).start()
            rs(i, 2).wait_recv()
            sum_out[i, 1] = (own[i, of(7), :] + f32(hop_in[i, 1])).astype(jnp.bfloat16)
            rs(i, 6).start()

        @pl.when((t >= 3) & (t < n + 3))
        def _():
            i = t - 3
            rs(i, 3).wait_recv()
            rs(i, 6).wait_recv()
            side_out[i] = (own[i, of(4), :] + f32(raw_in[i, 0]) + f32(sum_in[i, 1])).astype(jnp.bfloat16)
            rs(i, 7).start()

        @pl.when(t >= 4)
        def _():
            i = t - 4
            for k in (4, 5, 7):
                rs(i, k).wait_recv()
            done = own[i, of(0), :] + f32(raw_in[i, 1]) + f32(sum_in[i, 0]) + f32(side_in[i])
            for h in range(part):
                flat[pl.ds(i * part + h, block, stride=heads), :] = done[:, h * HEAD_DIM:(h + 1) * HEAD_DIM]

        return carry

    lax.fori_loop(0, n + 4, reduce_step, 0)

    back_out[...] = flat[...].reshape(block, heads, HEAD_DIM).astype(jnp.bfloat16)

    def back(k):
        return pltpu.make_async_remote_copy(
            back_out.at[pl.ds(peer(k) * most, most)], back_in.at[pl.ds(g * most, most)],
            re_send.at[k], re_recv.at[k], device_id=(s, peer(k), c), device_id_type=MESH,
        )

    for k in range(1, experts):
        back(k).start()
    mine = pltpu.make_async_copy(
        back_out.at[pl.ds(g * most, most)], back_in.at[pl.ds(g * most, most)], loc_sem.at[1]
    )
    mine.start()

    def drain(i, carry):
        for j in range(8):
            ag(i, j).wait_send()
            rs(i, j).wait_send()
        return carry

    lax.fori_loop(0, n, drain, 0)
    for k in range(1, experts):
        go(k).wait_send()
        back(k).wait_send()
    mine.wait()
    for k in range(1, experts):
        back(k).wait_recv()
    ret[...] = back_in[...]


def run_experts(outgoing, gate_w, up_w, down_w):
    total, heads, _ = outgoing.shape
    depth, hidden = gate_w.shape
    n = CHUNKS
    width = depth // n
    height = 16 * total
    half = height // 2
    bf16, f32 = jnp.bfloat16, jnp.float32
    dma = pltpu.SemaphoreType.DMA
    return pl.pallas_call(
        expert_kernel,
        out_shape=jax.ShapeDtypeStruct(outgoing.shape, bf16),
        in_specs=[pl.BlockSpec(memory_space=pltpu.VMEM)] + [pl.BlockSpec(memory_space=pl.ANY)] * 3,
        out_specs=pl.BlockSpec(memory_space=pltpu.VMEM),
        scratch_shapes=[
            pltpu.VMEM((n, width, hidden), bf16),
            pltpu.VMEM((n, width, hidden), bf16),
            pltpu.VMEM((n, hidden, width), bf16),
            pltpu.VMEM(outgoing.shape, bf16),
            pltpu.VMEM((total * heads, HEAD_DIM), f32),
            pltpu.VMEM((n, height, width), bf16),
            pltpu.VMEM((height, hidden), f32),
            pltpu.VMEM((height, hidden), f32),
            pltpu.VMEM((height, hidden), bf16),
            pltpu.VMEM((n, half, width), f32),
            pltpu.VMEM((n, half, width), bf16),
            pltpu.VMEM((n, half, width), bf16),
            pltpu.VMEM((n, 4, total, width), bf16),
            pltpu.VMEM((n, 2, total, width), bf16),
            pltpu.VMEM((n, 2, total, width), bf16),
            pltpu.VMEM((n, 2, total, width), bf16),
            pltpu.VMEM((n, 2, total, width), bf16),
            pltpu.VMEM((n, total, width), bf16),
            pltpu.VMEM((n, total, width), bf16),
            pltpu.VMEM(outgoing.shape, bf16),
            pltpu.VMEM(outgoing.shape, bf16),
            dma((3, n)),
            dma((2,)),
            dma((8,)),
            dma((8,)),
            dma((n, 8)),
            dma((n, 8)),
            dma((n, 8)),
            dma((n, 8)),
            dma((8,)),
            dma((8,)),
        ],
        compiler_params=pltpu.CompilerParams(
            collective_id=0, has_side_effects=True, vmem_limit_bytes=50 * 1024 * 1024
        ),
        name="experts",
    )(outgoing, gate_w, up_w, down_w)


def local(
    query,
    k_cache,
    v_cache,
    new_key,
    new_value,
    lengths,
    residual,
    norm_gain,
    router,
    routes,
    w_gate,
    w_up,
    w_down,
):
    rows = query.shape[0]
    width = query.shape[1]
    experts = lax.axis_size("grp")
    most = max(2, 2 * rows // experts)
    attended = attend(query, k_cache, v_cache, new_key, new_value, lengths)
    mixed = residual.astype(jnp.float32) + attended
    power = jnp.mean(mixed * mixed, axis=1, keepdims=True)
    normed = (mixed * lax.rsqrt(power + 1e-05) * norm_gain.astype(jnp.float32)).astype(jnp.bfloat16)
    logits = jnp.dot(normed, router, preferred_element_type=jnp.float32)
    chosen = routes[:, :, None] == jnp.arange(experts)[None, None, :]
    picked = jnp.sum(jnp.where(chosen, logits[:, None, :], 0.0), axis=-1)
    first = jax.nn.sigmoid(picked[:, 0] - picked[:, 1])
    second = jax.nn.sigmoid(picked[:, 1] - picked[:, 0])
    weights = jnp.stack([first, second], axis=1)
    ranks = slot_ranks(routes)
    slot_of = routes * most + ranks
    slot_range = jnp.arange(experts * most)
    placing = slot_of[:, :, None] == slot_range[None, None, :]
    one_hot = jnp.sum(placing.astype(jnp.float32), axis=1).astype(jnp.bfloat16)
    outgoing = jnp.einsum("rj,rx->jx", one_hot, normed, preferred_element_type=jnp.float32).astype(
        jnp.bfloat16
    )
    returned = run_experts(
        outgoing.reshape(experts * most, Q_HEADS, HEAD_DIM), w_gate[0], w_up[0], w_down[0]
    )
    returned = returned.reshape(experts * most, width).astype(jnp.float32)
    mixing = jnp.sum(jnp.where(placing, weights[:, :, None], 0.0), axis=1)
    combined = jnp.dot(
        mixing, returned, precision=lax.Precision.HIGHEST, preferred_element_type=jnp.float32
    )
    return (mixed + combined).astype(jnp.bfloat16)


def solution(mesh):
    placed = (
        P(("side", "grp", "cuts"), None),
        P(("side", "grp", "cuts"), None, None),
        P(("side", "grp", "cuts"), None, None),
        P(("side", "grp", "cuts"), None),
        P(("side", "grp", "cuts"), None),
        P(("side", "grp", "cuts")),
        P(("side", "grp", "cuts"), None),
        P(),
        P(),
        P(("side", "grp", "cuts"), None),
        P("grp", None, ("side", "cuts")),
        P("grp", None, ("side", "cuts")),
        P("grp", ("side", "cuts"), None),
    )
    return jax.shard_map(
        local,
        mesh=mesh,
        in_specs=placed,
        out_specs=P(("side", "grp", "cuts"), None),
        check_vma=False,
    )
```

```python
import math

import jax
import jax.numpy as jnp
from jax import lax
from jax.experimental import pallas as pl
from jax.experimental.pallas import tpu as pltpu
from jax.sharding import PartitionSpec as P

Q_HEADS = 48
KV_HEADS = 8
HEAD_DIM = 128
CHUNKS = 8
MESH = pl.DeviceIdType.MESH


def attend(query, k_cache, v_cache, new_key, new_value, lengths):
    rows, span, _ = k_cache.shape
    group = Q_HEADS // KV_HEADS
    scale = 1.0 / math.sqrt(HEAD_DIM)
    queries = query.reshape(rows, KV_HEADS, group, HEAD_DIM)
    keys = k_cache.reshape(rows, span, KV_HEADS, HEAD_DIM)
    values = v_cache.reshape(rows, span, KV_HEADS, HEAD_DIM)
    fresh_key = new_key.reshape(rows, KV_HEADS, HEAD_DIM)
    fresh_value = new_value.astype(jnp.float32).reshape(rows, KV_HEADS, 1, HEAD_DIM)
    old = jnp.einsum("rkgd,rskd->rkgs", queries, keys, preferred_element_type=jnp.float32) * scale
    own = (
        jnp.einsum("rkgd,rkd->rkg", queries, fresh_key, preferred_element_type=jnp.float32) * scale
    )
    live = jnp.arange(span)[None, :] < lengths[:, None]
    old = jnp.where(live[:, None, None, :], old, -jnp.inf)
    top = jnp.maximum(jnp.max(old, axis=-1), own)
    e_old = jnp.exp(old - top[..., None])
    e_own = jnp.exp(own - top)
    total = jnp.sum(e_old, axis=-1) + e_own
    p_old = (e_old / total[..., None]).astype(jnp.bfloat16)
    p_own = (e_own / total).astype(jnp.bfloat16).astype(jnp.float32)
    out = jnp.einsum("rkgs,rskd->rkgd", p_old, values, preferred_element_type=jnp.float32)
    out = out + p_own[..., None] * fresh_value
    return out.reshape(rows, Q_HEADS * HEAD_DIM)


def slot_ranks(block):
    flat = block.reshape(-1)
    order = jnp.arange(flat.shape[0])
    same = (flat[:, None] == flat[None, :]) & (order[None, :] < order[:, None])
    return jnp.sum(same.astype(jnp.int32), axis=1).reshape(block.shape)


def expert_kernel(
    slots, wg_hbm, wu_hbm, wd_hbm, ret,
    wg, wu, wd, arrived, flat, rows_in, gate, upper, act,
    own, pair_out, pair_in, raw_out, hop_in, raw_in, sum_out, sum_in, side_out, side_in,
    back_out, back_in,
    w_sem, loc_sem, go_send, go_recv, ag_send, ag_recv, rs_send, rs_recv, re_send, re_recv,
):
    n, height, width = rows_in.shape
    half = height // 2
    heads = slots.shape[1]
    part = heads // n
    most = 2
    experts = lax.axis_size("grp")
    block = experts * most
    s, g, c = lax.axis_index("side"), lax.axis_index("grp"), lax.axis_index("cuts")
    x, core = c // 2, lax.rem(c, 2)
    other = (1 - s, g, c)
    right = (s, g, lax.rem(x + 1, 4) * 2 + core)
    left = (s, g, lax.rem(x + 3, 4) * 2 + core)
    mate = (s, g, x * 2 + 1 - core)

    def peer(k):
        return lax.rem(g + k, experts)

    loads = []
    for i in range(n):
        loads.append((
            pltpu.make_async_copy(wg_hbm.at[pl.ds(i * width, width), :], wg.at[i], w_sem.at[0, i]),
            pltpu.make_async_copy(wu_hbm.at[pl.ds(i * width, width), :], wu.at[i], w_sem.at[1, i]),
        ))
    for i in range(n):
        loads.append((
            pltpu.make_async_copy(wd_hbm.at[:, pl.ds(i * width, width)], wd.at[i], w_sem.at[2, i]),
        ))
    for group in loads:
        for copy in group:
            copy.start()

    barrier = pltpu.get_barrier_semaphore()
    for k in range(1, experts):
        pl.semaphore_signal(barrier, inc=1, device_id=(s, peer(k), c), device_id_type=MESH)
    for device in (other, right, left, mate):
        pl.semaphore_signal(barrier, inc=1, device_id=device, device_id_type=MESH)
    pl.semaphore_wait(barrier, experts + 3)

    def go(k):
        return pltpu.make_async_remote_copy(
            slots.at[pl.ds(peer(k) * most, most)], arrived.at[pl.ds(g * most, most)],
            go_send.at[k], go_recv.at[k], device_id=(s, peer(k), c), device_id_type=MESH,
        )

    for k in range(1, experts):
        go(k).start()
    mine = pltpu.make_async_copy(
        slots.at[pl.ds(g * most, most)], arrived.at[pl.ds(g * most, most)], loc_sem.at[0]
    )
    mine.start()
    gate[...] = jnp.zeros_like(gate)
    upper[...] = jnp.zeros_like(upper)
    mine.wait()
    for k in range(1, experts):
        go(k).wait_recv()

    flat[...] = arrived[...].reshape(block * heads, HEAD_DIM).astype(jnp.float32)
    for h in range(heads):
        rows_in[h // part, 0:block, (h % part) * HEAD_DIM:(h % part + 1) * HEAD_DIM] = flat[
            pl.ds(h, block, stride=heads), :
        ].astype(jnp.bfloat16)

    table = (
        (0, 4, other), (0, 3, right), (0, 1, left), (4, 7, right), (4, 5, left), (3, 2, right), (5, 6, left),
    )

    def ag(i, j):
        if j == 7:
            src, dst, device = pl.ds(0, half), pl.ds(half, half), mate
        else:
            a, b, device = table[j]
            src, dst = pl.ds(a * block, block), pl.ds(b * block, block)
        return pltpu.make_async_remote_copy(
            rows_in.at[i, src, :], rows_in.at[i, dst, :], ag_send.at[i, j], ag_recv.at[i, j],
            device_id=device, device_id_type=MESH,
        )

    def first(i):
        for j in (0, 1, 2):
            ag(i, j).start()

    ahead = 3
    for i in range(ahead):
        first(i)

    def gather_step(t, carry):
        @pl.when(t + ahead < n)
        def _():
            first(t + ahead)

        @pl.when(t < n)
        def _():
            ag(t, 0).wait_recv()
            ag(t, 3).start()
            ag(t, 4).start()
            ag(t, 1).wait_recv()
            ag(t, 5).start()

        @pl.when((t >= 2) & (t < n + 2))
        def _():
            ag(t - 2, 4).wait_recv()
            ag(t - 2, 6).start()

        @pl.when((t >= 4) & (t < n + 4))
        def _():
            for j in (2, 3, 5, 6):
                ag(t - 4, j).wait_recv()
            ag(t - 4, 7).start()

        @pl.when(t >= 5)
        def _():
            i = t - 5
            ag(i, 7).wait_recv()
            pltpu.make_async_copy(wg_hbm.at[pl.ds(0, width), :], wg.at[i], w_sem.at[0, i]).wait()
            pltpu.make_async_copy(wu_hbm.at[pl.ds(0, width), :], wu.at[i], w_sem.at[1, i]).wait()
            gate[...] += jnp.dot(rows_in[i], wg[i], preferred_element_type=jnp.float32)
            upper[...] += jnp.dot(rows_in[i], wu[i], preferred_element_type=jnp.float32)

        return carry

    lax.fori_loop(0, n + 5, gather_step, 0)
    v = gate[...]
    act[...] = (v / (1.0 + jnp.exp(-v)) * upper[...]).astype(jnp.bfloat16)

    def rs(i, k):
        src, dst, device = (
            (pair_out.at[i], pair_in.at[i], mate),
            (raw_out.at[i, 0], hop_in.at[i, 0], right),
            (raw_out.at[i, 1], hop_in.at[i, 1], left),
            (raw_out.at[i, 2], raw_in.at[i, 0], right),
            (raw_out.at[i, 3], raw_in.at[i, 1], left),
            (sum_out.at[i, 0], sum_in.at[i, 0], right),
            (sum_out.at[i, 1], sum_in.at[i, 1], left),
            (side_out.at[i], side_in.at[i], other),
        )[k]
        return pltpu.make_async_remote_copy(
            src, dst, rs_send.at[i, k], rs_recv.at[i, k], device_id=device, device_id_type=MESH
        )

    def of(k):
        return pl.ds(k * block, block)

    def f32(value):
        return value.astype(jnp.float32)

    def reduce_step(t, carry):
        @pl.when(t < n)
        def _():
            pltpu.make_async_copy(wd_hbm.at[:, pl.ds(0, width)], wd.at[t], w_sem.at[2, t]).wait()
            product = jnp.dot(act[...], wd[t], preferred_element_type=jnp.float32)
            pair_out[t] = product[half:].astype(jnp.bfloat16)
            own[t] = product[:half]
            rs(t, 0).start()

        @pl.when((t >= 1) & (t < n + 1))
        def _():
            i = t - 1
            rs(i, 0).wait_recv()
            total = own[i] + f32(pair_in[i])
            for place, k in enumerate((2, 6, 5, 3)):
                raw_out[i, place] = total[k * block:(k + 1) * block].astype(jnp.bfloat16)
            own[i] = total
            for k in (1, 2, 3, 4):
                rs(i, k).start()

        @pl.when((t >= 3) & (t < n + 3))
        def _():
            i = t - 3
            rs(i, 1).wait_recv()
            sum_out[i, 0] = (own[i, of(1), :] + f32(hop_in[i, 0])).astype(jnp.bfloat16)
            rs(i, 5).start()
            rs(i, 2).wait_recv()
            sum_out[i, 1] = (own[i, of(7), :] + f32(hop_in[i, 1])).astype(jnp.bfloat16)
            rs(i, 6).start()

        @pl.when((t >= 5) & (t < n + 5))
        def _():
            i = t - 5
            rs(i, 3).wait_recv()
            rs(i, 6).wait_recv()
            side_out[i] = (own[i, of(4), :] + f32(raw_in[i, 0]) + f32(sum_in[i, 1])).astype(jnp.bfloat16)
            rs(i, 7).start()

        @pl.when(t >= 7)
        def _():
            i = t - 7
            for k in (4, 5, 7):
                rs(i, k).wait_recv()
            done = own[i, of(0), :] + f32(raw_in[i, 1]) + f32(sum_in[i, 0]) + f32(side_in[i])
            for h in range(part):
                flat[pl.ds(i * part + h, block, stride=heads), :] = done[:, h * HEAD_DIM:(h + 1) * HEAD_DIM]

        return carry

    lax.fori_loop(0, n + 7, reduce_step, 0)

    back_out[...] = flat[...].reshape(block, heads, HEAD_DIM).astype(jnp.bfloat16)

    def back(k):
        return pltpu.make_async_remote_copy(
            back_out.at[pl.ds(peer(k) * most, most)], back_in.at[pl.ds(g * most, most)],
            re_send.at[k], re_recv.at[k], device_id=(s, peer(k), c), device_id_type=MESH,
        )

    for k in range(1, experts):
        back(k).start()
    mine = pltpu.make_async_copy(
        back_out.at[pl.ds(g * most, most)], back_in.at[pl.ds(g * most, most)], loc_sem.at[1]
    )
    mine.start()

    def drain(i, carry):
        for j in range(8):
            ag(i, j).wait_send()
            rs(i, j).wait_send()
        return carry

    lax.fori_loop(0, n, drain, 0)
    for k in range(1, experts):
        go(k).wait_send()
        back(k).wait_send()
    mine.wait()
    for k in range(1, experts):
        back(k).wait_recv()
    ret[...] = back_in[...]


def run_experts(outgoing, gate_w, up_w, down_w):
    total, heads, _ = outgoing.shape
    depth, hidden = gate_w.shape
    n = CHUNKS
    width = depth // n
    height = 16 * total
    half = height // 2
    bf16, f32 = jnp.bfloat16, jnp.float32
    dma = pltpu.SemaphoreType.DMA
    return pl.pallas_call(
        expert_kernel,
        out_shape=jax.ShapeDtypeStruct(outgoing.shape, bf16),
        in_specs=[pl.BlockSpec(memory_space=pltpu.VMEM)] + [pl.BlockSpec(memory_space=pl.ANY)] * 3,
        out_specs=pl.BlockSpec(memory_space=pltpu.VMEM),
        scratch_shapes=[
            pltpu.VMEM((n, width, hidden), bf16),
            pltpu.VMEM((n, width, hidden), bf16),
            pltpu.VMEM((n, hidden, width), bf16),
            pltpu.VMEM(outgoing.shape, bf16),
            pltpu.VMEM((total * heads, HEAD_DIM), f32),
            pltpu.VMEM((n, height, width), bf16),
            pltpu.VMEM((height, hidden), f32),
            pltpu.VMEM((height, hidden), f32),
            pltpu.VMEM((height, hidden), bf16),
            pltpu.VMEM((n, half, width), f32),
            pltpu.VMEM((n, half, width), bf16),
            pltpu.VMEM((n, half, width), bf16),
            pltpu.VMEM((n, 4, total, width), bf16),
            pltpu.VMEM((n, 2, total, width), bf16),
            pltpu.VMEM((n, 2, total, width), bf16),
            pltpu.VMEM((n, 2, total, width), bf16),
            pltpu.VMEM((n, 2, total, width), bf16),
            pltpu.VMEM((n, total, width), bf16),
            pltpu.VMEM((n, total, width), bf16),
            pltpu.VMEM(outgoing.shape, bf16),
            pltpu.VMEM(outgoing.shape, bf16),
            dma((3, n)),
            dma((2,)),
            dma((8,)),
            dma((8,)),
            dma((n, 8)),
            dma((n, 8)),
            dma((n, 8)),
            dma((n, 8)),
            dma((8,)),
            dma((8,)),
        ],
        compiler_params=pltpu.CompilerParams(
            collective_id=0, has_side_effects=True, vmem_limit_bytes=50 * 1024 * 1024
        ),
        name="experts",
    )(outgoing, gate_w, up_w, down_w)


def local(
    query,
    k_cache,
    v_cache,
    new_key,
    new_value,
    lengths,
    residual,
    norm_gain,
    router,
    routes,
    w_gate,
    w_up,
    w_down,
):
    rows = query.shape[0]
    width = query.shape[1]
    experts = lax.axis_size("grp")
    most = max(2, 2 * rows // experts)
    attended = attend(query, k_cache, v_cache, new_key, new_value, lengths)
    mixed = residual.astype(jnp.float32) + attended
    power = jnp.mean(mixed * mixed, axis=1, keepdims=True)
    normed = (mixed * lax.rsqrt(power + 1e-05) * norm_gain.astype(jnp.float32)).astype(jnp.bfloat16)
    logits = jnp.dot(normed, router, preferred_element_type=jnp.float32)
    chosen = routes[:, :, None] == jnp.arange(experts)[None, None, :]
    picked = jnp.sum(jnp.where(chosen, logits[:, None, :], 0.0), axis=-1)
    first = jax.nn.sigmoid(picked[:, 0] - picked[:, 1])
    second = jax.nn.sigmoid(picked[:, 1] - picked[:, 0])
    weights = jnp.stack([first, second], axis=1)
    ranks = slot_ranks(routes)
    slot_of = routes * most + ranks
    slot_range = jnp.arange(experts * most)
    placing = slot_of[:, :, None] == slot_range[None, None, :]
    one_hot = jnp.sum(placing.astype(jnp.float32), axis=1).astype(jnp.bfloat16)
    outgoing = jnp.einsum("rj,rx->jx", one_hot, normed, preferred_element_type=jnp.float32).astype(
        jnp.bfloat16
    )
    returned = run_experts(
        outgoing.reshape(experts * most, Q_HEADS, HEAD_DIM), w_gate[0], w_up[0], w_down[0]
    )
    returned = returned.reshape(experts * most, width).astype(jnp.float32)
    mixing = jnp.sum(jnp.where(placing, weights[:, :, None], 0.0), axis=1)
    combined = jnp.dot(
        mixing, returned, precision=lax.Precision.HIGHEST, preferred_element_type=jnp.float32
    )
    return (mixed + combined).astype(jnp.bfloat16)


def solution(mesh):
    placed = (
        P(("side", "grp", "cuts"), None),
        P(("side", "grp", "cuts"), None, None),
        P(("side", "grp", "cuts"), None, None),
        P(("side", "grp", "cuts"), None),
        P(("side", "grp", "cuts"), None),
        P(("side", "grp", "cuts")),
        P(("side", "grp", "cuts"), None),
        P(),
        P(),
        P(("side", "grp", "cuts"), None),
        P("grp", None, ("side", "cuts")),
        P("grp", None, ("side", "cuts")),
        P("grp", ("side", "cuts"), None),
    )
    return jax.shard_map(
        local,
        mesh=mesh,
        in_specs=placed,
        out_specs=P(("side", "grp", "cuts"), None),
        check_vma=False,
    )
```

```python
import math

import jax
import jax.numpy as jnp
from jax import lax
from jax.experimental import pallas as pl
from jax.experimental.pallas import tpu as pltpu
from jax.sharding import PartitionSpec as P

Q_HEADS = 48
KV_HEADS = 8
HEAD_DIM = 128
CHUNKS = 8
MESH = pl.DeviceIdType.MESH


def attend(query, k_cache, v_cache, new_key, new_value, lengths):
    rows, span, _ = k_cache.shape
    group = Q_HEADS // KV_HEADS
    scale = 1.0 / math.sqrt(HEAD_DIM)
    queries = query.reshape(rows, KV_HEADS, group, HEAD_DIM)
    keys = k_cache.reshape(rows, span, KV_HEADS, HEAD_DIM)
    values = v_cache.reshape(rows, span, KV_HEADS, HEAD_DIM)
    fresh_key = new_key.reshape(rows, KV_HEADS, HEAD_DIM)
    fresh_value = new_value.astype(jnp.float32).reshape(rows, KV_HEADS, 1, HEAD_DIM)
    old = jnp.einsum("rkgd,rskd->rkgs", queries, keys, preferred_element_type=jnp.float32) * scale
    own = (
        jnp.einsum("rkgd,rkd->rkg", queries, fresh_key, preferred_element_type=jnp.float32) * scale
    )
    live = jnp.arange(span)[None, :] < lengths[:, None]
    old = jnp.where(live[:, None, None, :], old, -jnp.inf)
    top = jnp.maximum(jnp.max(old, axis=-1), own)
    e_old = jnp.exp(old - top[..., None])
    e_own = jnp.exp(own - top)
    total = jnp.sum(e_old, axis=-1) + e_own
    p_old = (e_old / total[..., None]).astype(jnp.bfloat16)
    p_own = (e_own / total).astype(jnp.bfloat16).astype(jnp.float32)
    out = jnp.einsum("rkgs,rskd->rkgd", p_old, values, preferred_element_type=jnp.float32)
    out = out + p_own[..., None] * fresh_value
    return out.reshape(rows, Q_HEADS * HEAD_DIM)


def slot_ranks(block):
    flat = block.reshape(-1)
    order = jnp.arange(flat.shape[0])
    same = (flat[:, None] == flat[None, :]) & (order[None, :] < order[:, None])
    return jnp.sum(same.astype(jnp.int32), axis=1).reshape(block.shape)


def expert_kernel(
    slots, wg_hbm, wu_hbm, wd_hbm, ret,
    wg, wu, wd, arrived, flat, rows_in, gate, upper, act,
    own, pair_out, pair_in, raw_out, hop_in, raw_in, sum_out, sum_in, side_out, side_in,
    back_out, back_in,
    w_sem, loc_sem, go_send, go_recv, ag_send, ag_recv, rs_send, rs_recv, re_send, re_recv,
):
    n, height, width = rows_in.shape
    half = height // 2
    heads = slots.shape[1]
    part = heads // n
    most = 2
    experts = lax.axis_size("grp")
    block = experts * most
    s, g, c = lax.axis_index("side"), lax.axis_index("grp"), lax.axis_index("cuts")
    x, core = c // 2, lax.rem(c, 2)
    other = (1 - s, g, c)
    right = (s, g, lax.rem(x + 1, 4) * 2 + core)
    left = (s, g, lax.rem(x + 3, 4) * 2 + core)
    mate = (s, g, x * 2 + 1 - core)

    def forward(i):
        return (s, g, lax.rem(x + 1 + 2 * lax.rem(i, 2), 4) * 2 + core)

    def backward(i):
        return (s, g, lax.rem(x + 3 + 2 * lax.rem(i, 2), 4) * 2 + core)

    def peer(k):
        return lax.rem(g + k, experts)

    loads = []
    for i in range(n):
        loads.append((
            pltpu.make_async_copy(wg_hbm.at[pl.ds(i * width, width), :], wg.at[i], w_sem.at[0, i]),
            pltpu.make_async_copy(wu_hbm.at[pl.ds(i * width, width), :], wu.at[i], w_sem.at[1, i]),
        ))
    for i in range(n):
        loads.append((
            pltpu.make_async_copy(wd_hbm.at[:, pl.ds(i * width, width)], wd.at[i], w_sem.at[2, i]),
        ))
    for group in loads:
        for copy in group:
            copy.start()

    barrier = pltpu.get_barrier_semaphore()
    for k in range(1, experts):
        pl.semaphore_signal(barrier, inc=1, device_id=(s, peer(k), c), device_id_type=MESH)
    for device in (other, right, left, mate):
        pl.semaphore_signal(barrier, inc=1, device_id=device, device_id_type=MESH)
    pl.semaphore_wait(barrier, experts + 3)

    def go(k):
        return pltpu.make_async_remote_copy(
            slots.at[pl.ds(peer(k) * most, most)], arrived.at[pl.ds(g * most, most)],
            go_send.at[k], go_recv.at[k], device_id=(s, peer(k), c), device_id_type=MESH,
        )

    for k in range(1, experts):
        go(k).start()
    mine = pltpu.make_async_copy(
        slots.at[pl.ds(g * most, most)], arrived.at[pl.ds(g * most, most)], loc_sem.at[0]
    )
    mine.start()
    gate[...] = jnp.zeros_like(gate)
    upper[...] = jnp.zeros_like(upper)
    mine.wait()
    for k in range(1, experts):
        go(k).wait_recv()

    flat[...] = arrived[...].reshape(block * heads, HEAD_DIM).astype(jnp.float32)
    for h in range(heads):
        rows_in[h // part, 0:block, (h % part) * HEAD_DIM:(h % part + 1) * HEAD_DIM] = flat[
            pl.ds(h, block, stride=heads), :
        ].astype(jnp.bfloat16)

    table = (
        (0, 4, other), (0, 3, right), (0, 1, left), (4, 7, right), (4, 5, left), None, (2, 6, other),
    )

    def ag(i, j):
        if j == 7:
            src, dst, device = pl.ds(0, half), pl.ds(half, half), mate
        elif j == 5:
            start = pl.multiple_of((3 - 2 * lax.rem(i, 2)) * block, block)
            src, dst, device = pl.ds(start, block), pl.ds(2 * block, block), forward(i)
        else:
            a, b, device = table[j]
            src, dst = pl.ds(a * block, block), pl.ds(b * block, block)
        return pltpu.make_async_remote_copy(
            rows_in.at[i, src, :], rows_in.at[i, dst, :], ag_send.at[i, j], ag_recv.at[i, j],
            device_id=device, device_id_type=MESH,
        )

    def first(i):
        for j in (0, 1, 2):
            ag(i, j).start()

    ahead = 3
    for i in range(ahead):
        first(i)

    def gather_step(t, carry):
        @pl.when(t + ahead < n)
        def _():
            first(t + ahead)

        @pl.when(t < n)
        def _():
            ag(t, 0).wait_recv()
            ag(t, 3).start()
            ag(t, 4).start()
            pltpu.make_async_copy(
                rows_in.at[t, 0:block, :], rows_in.at[t, 0:block, :], ag_recv.at[t, 1 + lax.rem(t, 2)]
            ).wait()
            ag(t, 5).start()

        @pl.when((t >= 2) & (t < n + 2))
        def _():
            ag(t - 2, 5).wait_recv()
            ag(t - 2, 6).start()

        @pl.when((t >= 4) & (t < n + 4))
        def _():
            pltpu.make_async_copy(
                rows_in.at[t - 4, 0:block, :], rows_in.at[t - 4, 0:block, :],
                ag_recv.at[t - 4, 2 - lax.rem(t, 2)],
            ).wait()
            for j in (3, 4, 6):
                ag(t - 4, j).wait_recv()
            ag(t - 4, 7).start()

        @pl.when(t >= 5)
        def _():
            i = t - 5
            ag(i, 7).wait_recv()
            pltpu.make_async_copy(wg_hbm.at[pl.ds(0, width), :], wg.at[i], w_sem.at[0, i]).wait()
            pltpu.make_async_copy(wu_hbm.at[pl.ds(0, width), :], wu.at[i], w_sem.at[1, i]).wait()
            gate[...] += jnp.dot(rows_in[i], wg[i], preferred_element_type=jnp.float32)
            upper[...] += jnp.dot(rows_in[i], wu[i], preferred_element_type=jnp.float32)

        return carry

    lax.fori_loop(0, n + 5, gather_step, 0)
    v = gate[...]
    act[...] = (v / (1.0 + jnp.exp(-v)) * upper[...]).astype(jnp.bfloat16)

    def rs(i, k):
        src, dst, device = (
            (pair_out.at[i], pair_in.at[i], mate),
            (raw_out.at[i, 0], hop_in.at[i], other),
            (raw_out.at[i, 1], raw_in.at[i, 0], right),
            (raw_out.at[i, 2], raw_in.at[i, 1], left),
            (raw_out.at[i, 3], raw_in.at[i, 2], backward(i)),
            (sum_out.at[i, 0], sum_in.at[i, 0], forward(i)),
            (sum_out.at[i, 1], sum_in.at[i, 1], forward(i)),
            (side_out.at[i], side_in.at[i], other),
        )[k]
        return pltpu.make_async_remote_copy(
            src, dst, rs_send.at[i, k], rs_recv.at[i, k], device_id=device, device_id_type=MESH
        )

    def of(k):
        return pl.ds(k * block, block)

    def f32(value):
        return value.astype(jnp.float32)

    def reduce_step(t, carry):
        @pl.when(t < n)
        def _():
            pltpu.make_async_copy(wd_hbm.at[:, pl.ds(0, width)], wd.at[t], w_sem.at[2, t]).wait()
            product = jnp.dot(act[...], wd[t], preferred_element_type=jnp.float32)
            pair_out[t] = product[half:].astype(jnp.bfloat16)
            own[t] = product[:half]
            rs(t, 0).start()

        @pl.when((t >= 1) & (t < n + 1))
        def _():
            i = t - 1
            rs(i, 0).wait_recv()
            total = own[i] + f32(pair_in[i])
            for place, k in enumerate((6, 5, 7)):
                raw_out[i, place] = total[k * block:(k + 1) * block].astype(jnp.bfloat16)
            own[i] = total
            near = pl.multiple_of((3 - 2 * lax.rem(i, 2)) * block, block)
            raw_out[i, 3] = own[i, pl.ds(near, block), :].astype(jnp.bfloat16)
            for k in (1, 2, 3, 4):
                rs(i, k).start()

        @pl.when((t >= 3) & (t < n + 3))
        def _():
            i = t - 3
            rs(i, 1).wait_recv()
            sum_out[i, 0] = (own[i, of(2), :] + f32(hop_in[i])).astype(jnp.bfloat16)
            rs(i, 5).start()
            rs(i, 2).wait_recv()
            rs(i, 3).wait_recv()
            side_out[i] = (own[i, of(4), :] + f32(raw_in[i, 0]) + f32(raw_in[i, 1])).astype(jnp.bfloat16)
            rs(i, 7).start()

        @pl.when((t >= 5) & (t < n + 5))
        def _():
            i = t - 5
            rs(i, 5).wait_recv()
            near = pl.multiple_of((1 + 2 * lax.rem(i, 2)) * block, block)
            sum_out[i, 1] = (own[i, pl.ds(near, block), :] + f32(sum_in[i, 0])).astype(jnp.bfloat16)
            rs(i, 6).start()

        @pl.when(t >= 7)
        def _():
            i = t - 7
            for k in (4, 6, 7):
                rs(i, k).wait_recv()
            done = own[i, of(0), :] + f32(raw_in[i, 2]) + f32(sum_in[i, 1]) + f32(side_in[i])
            for h in range(part):
                flat[pl.ds(i * part + h, block, stride=heads), :] = done[:, h * HEAD_DIM:(h + 1) * HEAD_DIM]

        return carry

    lax.fori_loop(0, n + 7, reduce_step, 0)

    back_out[...] = flat[...].reshape(block, heads, HEAD_DIM).astype(jnp.bfloat16)

    def back(k):
        return pltpu.make_async_remote_copy(
            back_out.at[pl.ds(peer(k) * most, most)], back_in.at[pl.ds(g * most, most)],
            re_send.at[k], re_recv.at[k], device_id=(s, peer(k), c), device_id_type=MESH,
        )

    for k in range(1, experts):
        back(k).start()
    mine = pltpu.make_async_copy(
        back_out.at[pl.ds(g * most, most)], back_in.at[pl.ds(g * most, most)], loc_sem.at[1]
    )
    mine.start()

    def drain(i, carry):
        for j in range(8):
            ag(i, j).wait_send()
            rs(i, j).wait_send()
        return carry

    lax.fori_loop(0, n, drain, 0)
    for k in range(1, experts):
        go(k).wait_send()
        back(k).wait_send()
    mine.wait()
    for k in range(1, experts):
        back(k).wait_recv()
    ret[...] = back_in[...]


def run_experts(outgoing, gate_w, up_w, down_w):
    total, heads, _ = outgoing.shape
    depth, hidden = gate_w.shape
    n = CHUNKS
    width = depth // n
    height = 16 * total
    half = height // 2
    bf16, f32 = jnp.bfloat16, jnp.float32
    dma = pltpu.SemaphoreType.DMA
    return pl.pallas_call(
        expert_kernel,
        out_shape=jax.ShapeDtypeStruct(outgoing.shape, bf16),
        in_specs=[pl.BlockSpec(memory_space=pltpu.VMEM)] + [pl.BlockSpec(memory_space=pl.ANY)] * 3,
        out_specs=pl.BlockSpec(memory_space=pltpu.VMEM),
        scratch_shapes=[
            pltpu.VMEM((n, width, hidden), bf16),
            pltpu.VMEM((n, width, hidden), bf16),
            pltpu.VMEM((n, hidden, width), bf16),
            pltpu.VMEM(outgoing.shape, bf16),
            pltpu.VMEM((total * heads, HEAD_DIM), f32),
            pltpu.VMEM((n, height, width), bf16),
            pltpu.VMEM((height, hidden), f32),
            pltpu.VMEM((height, hidden), f32),
            pltpu.VMEM((height, hidden), bf16),
            pltpu.VMEM((n, half, width), f32),
            pltpu.VMEM((n, half, width), bf16),
            pltpu.VMEM((n, half, width), bf16),
            pltpu.VMEM((n, 4, total, width), bf16),
            pltpu.VMEM((n, total, width), bf16),
            pltpu.VMEM((n, 3, total, width), bf16),
            pltpu.VMEM((n, 2, total, width), bf16),
            pltpu.VMEM((n, 2, total, width), bf16),
            pltpu.VMEM((n, total, width), bf16),
            pltpu.VMEM((n, total, width), bf16),
            pltpu.VMEM(outgoing.shape, bf16),
            pltpu.VMEM(outgoing.shape, bf16),
            dma((3, n)),
            dma((2,)),
            dma((8,)),
            dma((8,)),
            dma((n, 8)),
            dma((n, 8)),
            dma((n, 8)),
            dma((n, 8)),
            dma((8,)),
            dma((8,)),
        ],
        compiler_params=pltpu.CompilerParams(
            collective_id=0, has_side_effects=True, vmem_limit_bytes=50 * 1024 * 1024
        ),
        name="experts",
    )(outgoing, gate_w, up_w, down_w)


def local(
    query,
    k_cache,
    v_cache,
    new_key,
    new_value,
    lengths,
    residual,
    norm_gain,
    router,
    routes,
    w_gate,
    w_up,
    w_down,
):
    rows = query.shape[0]
    width = query.shape[1]
    experts = lax.axis_size("grp")
    most = max(2, 2 * rows // experts)
    attended = attend(query, k_cache, v_cache, new_key, new_value, lengths)
    mixed = residual.astype(jnp.float32) + attended
    power = jnp.mean(mixed * mixed, axis=1, keepdims=True)
    normed = (mixed * lax.rsqrt(power + 1e-05) * norm_gain.astype(jnp.float32)).astype(jnp.bfloat16)
    logits = jnp.dot(normed, router, preferred_element_type=jnp.float32)
    chosen = routes[:, :, None] == jnp.arange(experts)[None, None, :]
    picked = jnp.sum(jnp.where(chosen, logits[:, None, :], 0.0), axis=-1)
    first = jax.nn.sigmoid(picked[:, 0] - picked[:, 1])
    second = jax.nn.sigmoid(picked[:, 1] - picked[:, 0])
    weights = jnp.stack([first, second], axis=1)
    ranks = slot_ranks(routes)
    slot_of = routes * most + ranks
    slot_range = jnp.arange(experts * most)
    placing = slot_of[:, :, None] == slot_range[None, None, :]
    one_hot = jnp.sum(placing.astype(jnp.float32), axis=1).astype(jnp.bfloat16)
    outgoing = jnp.einsum("rj,rx->jx", one_hot, normed, preferred_element_type=jnp.float32).astype(
        jnp.bfloat16
    )
    returned = run_experts(
        outgoing.reshape(experts * most, Q_HEADS, HEAD_DIM), w_gate[0], w_up[0], w_down[0]
    )
    returned = returned.reshape(experts * most, width).astype(jnp.float32)
    mixing = jnp.sum(jnp.where(placing, weights[:, :, None], 0.0), axis=1)
    combined = jnp.dot(
        mixing, returned, precision=lax.Precision.HIGHEST, preferred_element_type=jnp.float32
    )
    return (mixed + combined).astype(jnp.bfloat16)


def solution(mesh):
    placed = (
        P(("side", "grp", "cuts"), None),
        P(("side", "grp", "cuts"), None, None),
        P(("side", "grp", "cuts"), None, None),
        P(("side", "grp", "cuts"), None),
        P(("side", "grp", "cuts"), None),
        P(("side", "grp", "cuts")),
        P(("side", "grp", "cuts"), None),
        P(),
        P(),
        P(("side", "grp", "cuts"), None),
        P("grp", None, ("side", "cuts")),
        P("grp", None, ("side", "cuts")),
        P("grp", ("side", "cuts"), None),
    )
    return jax.shard_map(
        local,
        mesh=mesh,
        in_specs=placed,
        out_specs=P(("side", "grp", "cuts"), None),
        check_vma=False,
    )
```

```python
import math

import jax
import jax.numpy as jnp
from jax import lax
from jax.experimental import pallas as pl
from jax.experimental.pallas import tpu as pltpu
from jax.sharding import PartitionSpec as P

Q_HEADS = 48
KV_HEADS = 8
HEAD_DIM = 128
CHUNKS = 12
PARTS = 3
MESH = pl.DeviceIdType.MESH


def attend(query, k_cache, v_cache, new_key, new_value, lengths):
    rows, span, _ = k_cache.shape
    group = Q_HEADS // KV_HEADS
    scale = 1.0 / math.sqrt(HEAD_DIM)
    queries = query.reshape(rows, KV_HEADS, group, HEAD_DIM)
    keys = k_cache.reshape(rows, span, KV_HEADS, HEAD_DIM)
    values = v_cache.reshape(rows, span, KV_HEADS, HEAD_DIM)
    fresh_key = new_key.reshape(rows, KV_HEADS, HEAD_DIM)
    fresh_value = new_value.astype(jnp.float32).reshape(rows, KV_HEADS, 1, HEAD_DIM)
    old = jnp.einsum("rkgd,rskd->rkgs", queries, keys, preferred_element_type=jnp.float32) * scale
    own = (
        jnp.einsum("rkgd,rkd->rkg", queries, fresh_key, preferred_element_type=jnp.float32) * scale
    )
    live = jnp.arange(span)[None, :] < lengths[:, None]
    old = jnp.where(live[:, None, None, :], old, -jnp.inf)
    top = jnp.maximum(jnp.max(old, axis=-1), own)
    e_old = jnp.exp(old - top[..., None])
    e_own = jnp.exp(own - top)
    total = jnp.sum(e_old, axis=-1) + e_own
    p_old = (e_old / total[..., None]).astype(jnp.bfloat16)
    p_own = (e_own / total).astype(jnp.bfloat16).astype(jnp.float32)
    out = jnp.einsum("rkgs,rskd->rkgd", p_old, values, preferred_element_type=jnp.float32)
    out = out + p_own[..., None] * fresh_value
    return out.reshape(rows, Q_HEADS * HEAD_DIM)


def slot_ranks(block):
    flat = block.reshape(-1)
    order = jnp.arange(flat.shape[0])
    same = (flat[:, None] == flat[None, :]) & (order[None, :] < order[:, None])
    return jnp.sum(same.astype(jnp.int32), axis=1).reshape(block.shape)


def expert_kernel(
    slots, wg_hbm, wu_hbm, wd_hbm, ret,
    wg, wu, wd, arrived, flat, rows_in, gate, upper, act,
    own, pair_out, pair_in, raw_out, hop_in, raw_in, sum_out, sum_in, side_out, side_in,
    back_out, back_in,
    w_sem, loc_sem, go_send, go_recv, ag_send, ag_recv, rs_send, rs_recv, re_send, re_recv,
):
    n, height, width = rows_in.shape
    half = height // 2
    heads = slots.shape[1]
    part = heads // n
    most = 2
    experts = lax.axis_size("grp")
    block = experts * most
    span = heads // PARTS
    s, g, c = lax.axis_index("side"), lax.axis_index("grp"), lax.axis_index("cuts")
    x, core = c // 2, lax.rem(c, 2)
    other = (1 - s, g, c)
    right = (s, g, lax.rem(x + 1, 4) * 2 + core)
    left = (s, g, lax.rem(x + 3, 4) * 2 + core)
    mate = (s, g, x * 2 + 1 - core)

    def forward(i):
        return (s, g, lax.rem(x + 1 + 2 * lax.rem(i, 2), 4) * 2 + core)

    def backward(i):
        return (s, g, lax.rem(x + 3 + 2 * lax.rem(i, 2), 4) * 2 + core)

    def peer(k):
        return lax.rem(g + k, experts)

    loads = []
    for i in range(n):
        loads.append((
            pltpu.make_async_copy(wg_hbm.at[pl.ds(i * width, width), :], wg.at[i], w_sem.at[0, i]),
            pltpu.make_async_copy(wu_hbm.at[pl.ds(i * width, width), :], wu.at[i], w_sem.at[1, i]),
        ))
    for i in range(n):
        loads.append((
            pltpu.make_async_copy(wd_hbm.at[:, pl.ds(i * width, width)], wd.at[i], w_sem.at[2, i]),
        ))
    for group in loads:
        for copy in group:
            copy.start()

    barrier = pltpu.get_barrier_semaphore()
    for k in range(1, experts):
        pl.semaphore_signal(barrier, inc=1, device_id=(s, peer(k), c), device_id_type=MESH)
    for device in (other, right, left, mate):
        pl.semaphore_signal(barrier, inc=1, device_id=device, device_id_type=MESH)
    pl.semaphore_wait(barrier, experts + 3)

    def go(k, p):
        return pltpu.make_async_remote_copy(
            slots.at[pl.ds(peer(k) * most, most), pl.ds(p * span, span)],
            arrived.at[pl.ds(g * most, most), pl.ds(p * span, span)],
            go_send.at[p, k], go_recv.at[p, k], device_id=(s, peer(k), c), device_id_type=MESH,
        )

    for p in range(PARTS):
        for k in range(1, experts):
            go(k, p).start()
    mine = pltpu.make_async_copy(
        slots.at[pl.ds(g * most, most)], arrived.at[pl.ds(g * most, most)], loc_sem.at[0]
    )
    mine.start()
    gate[...] = jnp.zeros_like(gate)
    upper[...] = jnp.zeros_like(upper)
    mine.wait()

    def unpack(p):
        for k in range(1, experts):
            go(k, p).wait_recv()
        first_row = p * block * span
        flat[first_row:first_row + block * span, :] = (
            arrived[:, p * span:(p + 1) * span, :].astype(jnp.float32).reshape(block * span, HEAD_DIM)
        )
        for h in range(p * span, (p + 1) * span):
            rows_in[h // part, 0:block, (h % part) * HEAD_DIM:(h % part + 1) * HEAD_DIM] = flat[
                pl.ds(first_row + h % span, block, stride=span), :
            ].astype(jnp.bfloat16)

    unpack(0)

    table = (
        (0, 4, other), (0, 3, right), (0, 1, left), (4, 7, right), (4, 5, left), None, (2, 6, other),
    )

    def ag(i, j):
        if j == 7:
            src, dst, device = pl.ds(0, half), pl.ds(half, half), mate
        elif j == 5:
            start = pl.multiple_of((3 - 2 * lax.rem(i, 2)) * block, block)
            src, dst, device = pl.ds(start, block), pl.ds(2 * block, block), forward(i)
        else:
            a, b, device = table[j]
            src, dst = pl.ds(a * block, block), pl.ds(b * block, block)
        return pltpu.make_async_remote_copy(
            rows_in.at[i, src, :], rows_in.at[i, dst, :], ag_send.at[i, j], ag_recv.at[i, j],
            device_id=device, device_id_type=MESH,
        )

    def first(i):
        for j in (0, 1, 2):
            ag(i, j).start()

    ahead = 3
    for i in range(ahead):
        first(i)

    def gather_step(t, carry):
        for p in range(1, PARTS):
            @pl.when(t + ahead == p * span // part)
            def _(p=p):
                unpack(p)

        @pl.when(t + ahead < n)
        def _():
            first(t + ahead)

        @pl.when(t < n)
        def _():
            ag(t, 0).wait_recv()
            ag(t, 3).start()
            ag(t, 4).start()
            pltpu.make_async_copy(
                rows_in.at[t, 0:block, :], rows_in.at[t, 0:block, :], ag_recv.at[t, 1 + lax.rem(t, 2)]
            ).wait()
            ag(t, 5).start()

        @pl.when((t >= 2) & (t < n + 2))
        def _():
            ag(t - 2, 5).wait_recv()
            ag(t - 2, 6).start()

        @pl.when((t >= 4) & (t < n + 4))
        def _():
            pltpu.make_async_copy(
                rows_in.at[t - 4, 0:block, :], rows_in.at[t - 4, 0:block, :],
                ag_recv.at[t - 4, 2 - lax.rem(t, 2)],
            ).wait()
            for j in (3, 4, 6):
                ag(t - 4, j).wait_recv()
            ag(t - 4, 7).start()

        @pl.when(t >= 5)
        def _():
            i = t - 5
            ag(i, 7).wait_recv()
            pltpu.make_async_copy(wg_hbm.at[pl.ds(0, width), :], wg.at[i], w_sem.at[0, i]).wait()
            pltpu.make_async_copy(wu_hbm.at[pl.ds(0, width), :], wu.at[i], w_sem.at[1, i]).wait()
            gate[...] += jnp.dot(rows_in[i], wg[i], preferred_element_type=jnp.float32)
            upper[...] += jnp.dot(rows_in[i], wu[i], preferred_element_type=jnp.float32)

        return carry

    lax.fori_loop(0, n + 5, gather_step, 0)
    v = gate[...]
    act[...] = (v / (1.0 + jnp.exp(-v)) * upper[...]).astype(jnp.bfloat16)

    def rs(i, k):
        src, dst, device = (
            (pair_out.at[i], pair_in.at[i], mate),
            (raw_out.at[i, 0], hop_in.at[i], other),
            (raw_out.at[i, 1], raw_in.at[i, 0], right),
            (raw_out.at[i, 2], raw_in.at[i, 1], left),
            (raw_out.at[i, 3], raw_in.at[i, 2], backward(i)),
            (sum_out.at[i, 0], sum_in.at[i, 0], forward(i)),
            (sum_out.at[i, 1], sum_in.at[i, 1], forward(i)),
            (side_out.at[i], side_in.at[i], other),
        )[k]
        return pltpu.make_async_remote_copy(
            src, dst, rs_send.at[i, k], rs_recv.at[i, k], device_id=device, device_id_type=MESH
        )

    def of(k):
        return pl.ds(k * block, block)

    def f32(value):
        return value.astype(jnp.float32)

    def back(k, p):
        return pltpu.make_async_remote_copy(
            back_out.at[pl.ds(peer(k) * most, most), pl.ds(p * span, span)],
            back_in.at[pl.ds(g * most, most), pl.ds(p * span, span)],
            re_send.at[p, k], re_recv.at[p, k], device_id=(s, peer(k), c), device_id_type=MESH,
        )

    def reduce_step(t, carry):
        @pl.when(t < n)
        def _():
            pltpu.make_async_copy(wd_hbm.at[:, pl.ds(0, width)], wd.at[t], w_sem.at[2, t]).wait()
            product = jnp.dot(act[...], wd[t], preferred_element_type=jnp.float32)
            pair_out[t] = product[half:].astype(jnp.bfloat16)
            own[t] = product[:half]
            rs(t, 0).start()

        @pl.when((t >= 1) & (t < n + 1))
        def _():
            i = t - 1
            rs(i, 0).wait_recv()
            total = own[i] + f32(pair_in[i])
            for place, k in enumerate((6, 5, 7)):
                raw_out[i, place] = total[k * block:(k + 1) * block].astype(jnp.bfloat16)
            own[i] = total
            near = pl.multiple_of((3 - 2 * lax.rem(i, 2)) * block, block)
            raw_out[i, 3] = own[i, pl.ds(near, block), :].astype(jnp.bfloat16)
            for k in (1, 2, 3, 4):
                rs(i, k).start()

        @pl.when((t >= 3) & (t < n + 3))
        def _():
            i = t - 3
            rs(i, 1).wait_recv()
            sum_out[i, 0] = (own[i, of(2), :] + f32(hop_in[i])).astype(jnp.bfloat16)
            rs(i, 5).start()
            rs(i, 2).wait_recv()
            rs(i, 3).wait_recv()
            side_out[i] = (own[i, of(4), :] + f32(raw_in[i, 0]) + f32(raw_in[i, 1])).astype(jnp.bfloat16)
            rs(i, 7).start()

        @pl.when((t >= 5) & (t < n + 5))
        def _():
            i = t - 5
            rs(i, 5).wait_recv()
            near = pl.multiple_of((1 + 2 * lax.rem(i, 2)) * block, block)
            sum_out[i, 1] = (own[i, pl.ds(near, block), :] + f32(sum_in[i, 0])).astype(jnp.bfloat16)
            rs(i, 6).start()

        @pl.when(t >= 7)
        def _():
            i = t - 7
            for k in (4, 6, 7):
                rs(i, k).wait_recv()
            done = own[i, of(0), :] + f32(raw_in[i, 2]) + f32(sum_in[i, 1]) + f32(side_in[i])
            chunks = span // part
            place = (i // chunks) * (block * span) + lax.rem(i, chunks) * part
            for h in range(part):
                flat[pl.ds(place + h, block, stride=span), :] = done[:, h * HEAD_DIM:(h + 1) * HEAD_DIM]
            for p in range(PARTS):
                @pl.when(i == (p + 1) * chunks - 1)
                def _(p=p):
                    back_out[:, p * span:(p + 1) * span, :] = (
                        flat[p * block * span:(p + 1) * block * span, :]
                        .reshape(block, span, HEAD_DIM).astype(jnp.bfloat16)
                    )
                    for k in range(1, experts):
                        back(k, p).start()

        return carry

    lax.fori_loop(0, n + 7, reduce_step, 0)
    mine = pltpu.make_async_copy(
        back_out.at[pl.ds(g * most, most)], back_in.at[pl.ds(g * most, most)], loc_sem.at[1]
    )
    mine.start()

    def drain(i, carry):
        for j in range(8):
            ag(i, j).wait_send()
            rs(i, j).wait_send()
        return carry

    lax.fori_loop(0, n, drain, 0)
    for p in range(PARTS):
        for k in range(1, experts):
            go(k, p).wait_send()
            back(k, p).wait_send()
    mine.wait()
    for p in range(PARTS):
        for k in range(1, experts):
            back(k, p).wait_recv()
    ret[...] = back_in[...]


def run_experts(outgoing, gate_w, up_w, down_w):
    total, heads, _ = outgoing.shape
    depth, hidden = gate_w.shape
    n = CHUNKS
    width = depth // n
    height = 16 * total
    half = height // 2
    bf16, f32 = jnp.bfloat16, jnp.float32
    dma = pltpu.SemaphoreType.DMA
    return pl.pallas_call(
        expert_kernel,
        out_shape=jax.ShapeDtypeStruct(outgoing.shape, bf16),
        in_specs=[pl.BlockSpec(memory_space=pltpu.VMEM)] + [pl.BlockSpec(memory_space=pl.ANY)] * 3,
        out_specs=pl.BlockSpec(memory_space=pltpu.VMEM),
        scratch_shapes=[
            pltpu.VMEM((n, width, hidden), bf16),
            pltpu.VMEM((n, width, hidden), bf16),
            pltpu.VMEM((n, hidden, width), bf16),
            pltpu.VMEM(outgoing.shape, bf16),
            pltpu.VMEM((total * heads, HEAD_DIM), f32),
            pltpu.VMEM((n, height, width), bf16),
            pltpu.VMEM((height, hidden), f32),
            pltpu.VMEM((height, hidden), f32),
            pltpu.VMEM((height, hidden), bf16),
            pltpu.VMEM((n, half, width), f32),
            pltpu.VMEM((n, half, width), bf16),
            pltpu.VMEM((n, half, width), bf16),
            pltpu.VMEM((n, 4, total, width), bf16),
            pltpu.VMEM((n, total, width), bf16),
            pltpu.VMEM((n, 3, total, width), bf16),
            pltpu.VMEM((n, 2, total, width), bf16),
            pltpu.VMEM((n, 2, total, width), bf16),
            pltpu.VMEM((n, total, width), bf16),
            pltpu.VMEM((n, total, width), bf16),
            pltpu.VMEM(outgoing.shape, bf16),
            pltpu.VMEM(outgoing.shape, bf16),
            dma((3, n)),
            dma((2,)),
            dma((PARTS, 8)),
            dma((PARTS, 8)),
            dma((n, 8)),
            dma((n, 8)),
            dma((n, 8)),
            dma((n, 8)),
            dma((PARTS, 8)),
            dma((PARTS, 8)),
        ],
        compiler_params=pltpu.CompilerParams(
            collective_id=0, has_side_effects=True, vmem_limit_bytes=50 * 1024 * 1024
        ),
        name="experts",
    )(outgoing, gate_w, up_w, down_w)


def local(
    query,
    k_cache,
    v_cache,
    new_key,
    new_value,
    lengths,
    residual,
    norm_gain,
    router,
    routes,
    w_gate,
    w_up,
    w_down,
):
    rows = query.shape[0]
    width = query.shape[1]
    experts = lax.axis_size("grp")
    most = max(2, 2 * rows // experts)
    attended = attend(query, k_cache, v_cache, new_key, new_value, lengths)
    mixed = residual.astype(jnp.float32) + attended
    power = jnp.mean(mixed * mixed, axis=1, keepdims=True)
    normed = (mixed * lax.rsqrt(power + 1e-05) * norm_gain.astype(jnp.float32)).astype(jnp.bfloat16)
    logits = jnp.dot(normed, router, preferred_element_type=jnp.float32)
    chosen = routes[:, :, None] == jnp.arange(experts)[None, None, :]
    picked = jnp.sum(jnp.where(chosen, logits[:, None, :], 0.0), axis=-1)
    first = jax.nn.sigmoid(picked[:, 0] - picked[:, 1])
    second = jax.nn.sigmoid(picked[:, 1] - picked[:, 0])
    weights = jnp.stack([first, second], axis=1)
    ranks = slot_ranks(routes)
    slot_of = routes * most + ranks
    slot_range = jnp.arange(experts * most)
    placing = slot_of[:, :, None] == slot_range[None, None, :]
    one_hot = jnp.sum(placing.astype(jnp.float32), axis=1).astype(jnp.bfloat16)
    outgoing = jnp.einsum("rj,rx->jx", one_hot, normed, preferred_element_type=jnp.float32).astype(
        jnp.bfloat16
    )
    returned = run_experts(
        outgoing.reshape(experts * most, Q_HEADS, HEAD_DIM), w_gate[0], w_up[0], w_down[0]
    )
    returned = returned.reshape(experts * most, width).astype(jnp.float32)
    mixing = jnp.sum(jnp.where(placing, weights[:, :, None], 0.0), axis=1)
    combined = jnp.dot(
        mixing, returned, precision=lax.Precision.HIGHEST, preferred_element_type=jnp.float32
    )
    return (mixed + combined).astype(jnp.bfloat16)


def solution(mesh):
    placed = (
        P(("side", "grp", "cuts"), None),
        P(("side", "grp", "cuts"), None, None),
        P(("side", "grp", "cuts"), None, None),
        P(("side", "grp", "cuts"), None),
        P(("side", "grp", "cuts"), None),
        P(("side", "grp", "cuts")),
        P(("side", "grp", "cuts"), None),
        P(),
        P(),
        P(("side", "grp", "cuts"), None),
        P("grp", None, ("side", "cuts")),
        P("grp", None, ("side", "cuts")),
        P("grp", ("side", "cuts"), None),
    )
    return jax.shard_map(
        local,
        mesh=mesh,
        in_specs=placed,
        out_specs=P(("side", "grp", "cuts"), None),
        check_vma=False,
    )
```

```python
import math

import jax
import jax.numpy as jnp
from jax import lax
from jax.experimental import pallas as pl
from jax.experimental.pallas import tpu as pltpu
from jax.sharding import PartitionSpec as P

Q_HEADS = 48
KV_HEADS = 8
HEAD_DIM = 128
CHUNKS = 8
PARTS = 3
MESH = pl.DeviceIdType.MESH


def attend(query, k_cache, v_cache, new_key, new_value, lengths):
    rows, span, _ = k_cache.shape
    group = Q_HEADS // KV_HEADS
    scale = 1.0 / math.sqrt(HEAD_DIM)
    queries = query.reshape(rows, KV_HEADS, group, HEAD_DIM)
    keys = k_cache.reshape(rows, span, KV_HEADS, HEAD_DIM)
    values = v_cache.reshape(rows, span, KV_HEADS, HEAD_DIM)
    fresh_key = new_key.reshape(rows, KV_HEADS, HEAD_DIM)
    fresh_value = new_value.astype(jnp.float32).reshape(rows, KV_HEADS, 1, HEAD_DIM)
    old = jnp.einsum("rkgd,rskd->rkgs", queries, keys, preferred_element_type=jnp.float32) * scale
    own = (
        jnp.einsum("rkgd,rkd->rkg", queries, fresh_key, preferred_element_type=jnp.float32) * scale
    )
    live = jnp.arange(span)[None, :] < lengths[:, None]
    old = jnp.where(live[:, None, None, :], old, -jnp.inf)
    top = jnp.maximum(jnp.max(old, axis=-1), own)
    e_old = jnp.exp(old - top[..., None])
    e_own = jnp.exp(own - top)
    total = jnp.sum(e_old, axis=-1) + e_own
    p_old = (e_old / total[..., None]).astype(jnp.bfloat16)
    p_own = (e_own / total).astype(jnp.bfloat16).astype(jnp.float32)
    out = jnp.einsum("rkgs,rskd->rkgd", p_old, values, preferred_element_type=jnp.float32)
    out = out + p_own[..., None] * fresh_value
    return out.reshape(rows, Q_HEADS * HEAD_DIM)


def slot_ranks(block):
    flat = block.reshape(-1)
    order = jnp.arange(flat.shape[0])
    same = (flat[:, None] == flat[None, :]) & (order[None, :] < order[:, None])
    return jnp.sum(same.astype(jnp.int32), axis=1).reshape(block.shape)


def expert_kernel(
    slots, wg_hbm, wu_hbm, wd_hbm, ret,
    wg, wu, wd, arrived, flat, rows_in, gate, upper, act,
    own, pair_out, pair_in, raw_out, hop_in, raw_in, sum_out, sum_in, side_out, side_in,
    back_out, back_in,
    w_sem, loc_sem, go_send, go_recv, ag_send, ag_recv, rs_send, rs_recv, re_send, re_recv,
):
    n, height, width = rows_in.shape
    half = height // 2
    heads = slots.shape[1]
    part = heads // n
    most = 2
    experts = lax.axis_size("grp")
    block = experts * most
    span = heads // PARTS
    s, g, c = lax.axis_index("side"), lax.axis_index("grp"), lax.axis_index("cuts")
    x, core = c // 2, lax.rem(c, 2)
    other = (1 - s, g, c)
    right = (s, g, lax.rem(x + 1, 4) * 2 + core)
    left = (s, g, lax.rem(x + 3, 4) * 2 + core)
    mate = (s, g, x * 2 + 1 - core)

    def forward(i):
        return (s, g, lax.rem(x + 1 + 2 * lax.rem(i, 2), 4) * 2 + core)

    def backward(i):
        return (s, g, lax.rem(x + 3 + 2 * lax.rem(i, 2), 4) * 2 + core)

    def peer(k):
        return lax.rem(g + k, experts)

    loads = []
    for i in range(n):
        loads.append((
            pltpu.make_async_copy(wg_hbm.at[pl.ds(i * width, width), :], wg.at[i], w_sem.at[0, i]),
            pltpu.make_async_copy(wu_hbm.at[pl.ds(i * width, width), :], wu.at[i], w_sem.at[1, i]),
        ))
    for i in range(n):
        loads.append((
            pltpu.make_async_copy(wd_hbm.at[:, pl.ds(i * width, width)], wd.at[i], w_sem.at[2, i]),
        ))
    for group in loads:
        for copy in group:
            copy.start()

    barrier = pltpu.get_barrier_semaphore()
    for k in range(1, experts):
        pl.semaphore_signal(barrier, inc=1, device_id=(s, peer(k), c), device_id_type=MESH)
    for device in (other, right, left, mate):
        pl.semaphore_signal(barrier, inc=1, device_id=device, device_id_type=MESH)
    pl.semaphore_wait(barrier, experts + 3)

    def go(k, p):
        return pltpu.make_async_remote_copy(
            slots.at[pl.ds(peer(k) * most, most), pl.ds(p * span, span)],
            arrived.at[pl.ds(g * most, most), pl.ds(p * span, span)],
            go_send.at[p, k], go_recv.at[p, k], device_id=(s, peer(k), c), device_id_type=MESH,
        )

    for p in range(PARTS):
        for k in range(1, experts):
            go(k, p).start()
    mine = pltpu.make_async_copy(
        slots.at[pl.ds(g * most, most)], arrived.at[pl.ds(g * most, most)], loc_sem.at[0]
    )
    mine.start()
    gate[...] = jnp.zeros_like(gate)
    upper[...] = jnp.zeros_like(upper)
    mine.wait()

    def unpack(p):
        for k in range(1, experts):
            go(k, p).wait_recv()
        first_row = p * block * span
        flat[first_row:first_row + block * span, :] = (
            arrived[:, p * span:(p + 1) * span, :].astype(jnp.float32).reshape(block * span, HEAD_DIM)
        )
        for h in range(p * span, (p + 1) * span):
            rows_in[h // part, 0:block, (h % part) * HEAD_DIM:(h % part + 1) * HEAD_DIM] = flat[
                pl.ds(first_row + h % span, block, stride=span), :
            ].astype(jnp.bfloat16)

    unpack(0)

    table = (
        (0, 4, other), (0, 3, right), (0, 1, left), (4, 7, right), (4, 5, left), None, (2, 6, other),
    )

    def ag(i, j):
        if j == 7:
            src, dst, device = pl.ds(0, half), pl.ds(half, half), mate
        elif j == 5:
            start = pl.multiple_of((3 - 2 * lax.rem(i, 2)) * block, block)
            src, dst, device = pl.ds(start, block), pl.ds(2 * block, block), forward(i)
        else:
            a, b, device = table[j]
            src, dst = pl.ds(a * block, block), pl.ds(b * block, block)
        return pltpu.make_async_remote_copy(
            rows_in.at[i, src, :], rows_in.at[i, dst, :], ag_send.at[i, j], ag_recv.at[i, j],
            device_id=device, device_id_type=MESH,
        )

    def first(i):
        for j in (0, 1, 2):
            ag(i, j).start()

    ahead = 2
    for i in range(ahead):
        first(i)

    def gather_step(t, carry):
        for p in range(1, PARTS):
            @pl.when(t + ahead == p * span // part)
            def _(p=p):
                unpack(p)

        @pl.when(t + ahead < n)
        def _():
            first(t + ahead)

        @pl.when(t < n)
        def _():
            ag(t, 0).wait_recv()
            ag(t, 3).start()
            ag(t, 4).start()
            pltpu.make_async_copy(
                rows_in.at[t, 0:block, :], rows_in.at[t, 0:block, :], ag_recv.at[t, 1 + lax.rem(t, 2)]
            ).wait()
            ag(t, 5).start()

        @pl.when((t >= 2) & (t < n + 2))
        def _():
            ag(t - 2, 5).wait_recv()
            ag(t - 2, 6).start()

        @pl.when((t >= 4) & (t < n + 4))
        def _():
            pltpu.make_async_copy(
                rows_in.at[t - 4, 0:block, :], rows_in.at[t - 4, 0:block, :],
                ag_recv.at[t - 4, 2 - lax.rem(t, 2)],
            ).wait()
            for j in (3, 4, 6):
                ag(t - 4, j).wait_recv()
            ag(t - 4, 7).start()

        @pl.when(t >= 5)
        def _():
            i = t - 5
            ag(i, 7).wait_recv()
            pltpu.make_async_copy(wg_hbm.at[pl.ds(0, width), :], wg.at[i], w_sem.at[0, i]).wait()
            pltpu.make_async_copy(wu_hbm.at[pl.ds(0, width), :], wu.at[i], w_sem.at[1, i]).wait()
            gate[...] += jnp.dot(rows_in[i], wg[i], preferred_element_type=jnp.float32)
            upper[...] += jnp.dot(rows_in[i], wu[i], preferred_element_type=jnp.float32)

        return carry

    lax.fori_loop(0, n + 5, gather_step, 0)
    v = gate[...]
    act[...] = (v / (1.0 + jnp.exp(-v)) * upper[...]).astype(jnp.bfloat16)

    def rs(i, k):
        src, dst, device = (
            (pair_out.at[i], pair_in.at[i], mate),
            (raw_out.at[i, 0], hop_in.at[i], other),
            (raw_out.at[i, 1], raw_in.at[i, 0], right),
            (raw_out.at[i, 2], raw_in.at[i, 1], left),
            (raw_out.at[i, 3], raw_in.at[i, 2], backward(i)),
            (sum_out.at[i, 0], sum_in.at[i, 0], forward(i)),
            (sum_out.at[i, 1], sum_in.at[i, 1], forward(i)),
            (side_out.at[i], side_in.at[i], other),
        )[k]
        return pltpu.make_async_remote_copy(
            src, dst, rs_send.at[i, k], rs_recv.at[i, k], device_id=device, device_id_type=MESH
        )

    def of(k):
        return pl.ds(k * block, block)

    def f32(value):
        return value.astype(jnp.float32)

    def back(k, p):
        return pltpu.make_async_remote_copy(
            back_out.at[pl.ds(peer(k) * most, most), pl.ds(p * span, span)],
            back_in.at[pl.ds(g * most, most), pl.ds(p * span, span)],
            re_send.at[p, k], re_recv.at[p, k], device_id=(s, peer(k), c), device_id_type=MESH,
        )

    def reduce_step(t, carry):
        @pl.when(t < n)
        def _():
            pltpu.make_async_copy(wd_hbm.at[:, pl.ds(0, width)], wd.at[t], w_sem.at[2, t]).wait()
            product = jnp.dot(act[...], wd[t], preferred_element_type=jnp.float32)
            pair_out[t] = product[half:].astype(jnp.bfloat16)
            own[t] = product[:half]
            rs(t, 0).start()

        @pl.when((t >= 1) & (t < n + 1))
        def _():
            i = t - 1
            rs(i, 0).wait_recv()
            total = own[i] + f32(pair_in[i])
            for place, k in enumerate((6, 5, 7)):
                raw_out[i, place] = total[k * block:(k + 1) * block].astype(jnp.bfloat16)
            own[i] = total
            near = pl.multiple_of((3 - 2 * lax.rem(i, 2)) * block, block)
            raw_out[i, 3] = own[i, pl.ds(near, block), :].astype(jnp.bfloat16)
            for k in (1, 2, 3, 4):
                rs(i, k).start()

        @pl.when((t >= 3) & (t < n + 3))
        def _():
            i = t - 3
            rs(i, 1).wait_recv()
            sum_out[i, 0] = (own[i, of(2), :] + f32(hop_in[i])).astype(jnp.bfloat16)
            rs(i, 5).start()
            rs(i, 2).wait_recv()
            rs(i, 3).wait_recv()
            side_out[i] = (own[i, of(4), :] + f32(raw_in[i, 0]) + f32(raw_in[i, 1])).astype(jnp.bfloat16)
            rs(i, 7).start()

        @pl.when((t >= 5) & (t < n + 5))
        def _():
            i = t - 5
            rs(i, 5).wait_recv()
            near = pl.multiple_of((1 + 2 * lax.rem(i, 2)) * block, block)
            sum_out[i, 1] = (own[i, pl.ds(near, block), :] + f32(sum_in[i, 0])).astype(jnp.bfloat16)
            rs(i, 6).start()

        @pl.when(t >= 7)
        def _():
            i = t - 7
            for k in (4, 6, 7):
                rs(i, k).wait_recv()
            done = own[i, of(0), :] + f32(raw_in[i, 2]) + f32(sum_in[i, 1]) + f32(side_in[i])
            for h in range(part):
                head = i * part + h
                place = lax.div(head, span) * (block * span) + lax.rem(head, span)
                flat[pl.ds(place, block, stride=span), :] = done[:, h * HEAD_DIM:(h + 1) * HEAD_DIM]
            for p in range(PARTS):
                @pl.when(i == ((p + 1) * span - 1) // part)
                def _(p=p):
                    back_out[:, p * span:(p + 1) * span, :] = (
                        flat[p * block * span:(p + 1) * block * span, :]
                        .reshape(block, span, HEAD_DIM).astype(jnp.bfloat16)
                    )
                    for k in range(1, experts):
                        back(k, p).start()

        return carry

    lax.fori_loop(0, n + 7, reduce_step, 0)
    mine = pltpu.make_async_copy(
        back_out.at[pl.ds(g * most, most)], back_in.at[pl.ds(g * most, most)], loc_sem.at[1]
    )
    mine.start()

    def drain(i, carry):
        for j in range(8):
            ag(i, j).wait_send()
            rs(i, j).wait_send()
        return carry

    lax.fori_loop(0, n, drain, 0)
    for p in range(PARTS):
        for k in range(1, experts):
            go(k, p).wait_send()
            back(k, p).wait_send()
    mine.wait()
    for p in range(PARTS):
        for k in range(1, experts):
            back(k, p).wait_recv()
    ret[...] = back_in[...]


def run_experts(outgoing, gate_w, up_w, down_w):
    total, heads, _ = outgoing.shape
    depth, hidden = gate_w.shape
    n = CHUNKS
    width = depth // n
    height = 16 * total
    half = height // 2
    bf16, f32 = jnp.bfloat16, jnp.float32
    dma = pltpu.SemaphoreType.DMA
    return pl.pallas_call(
        expert_kernel,
        out_shape=jax.ShapeDtypeStruct(outgoing.shape, bf16),
        in_specs=[pl.BlockSpec(memory_space=pltpu.VMEM)] + [pl.BlockSpec(memory_space=pl.ANY)] * 3,
        out_specs=pl.BlockSpec(memory_space=pltpu.VMEM),
        scratch_shapes=[
            pltpu.VMEM((n, width, hidden), bf16),
            pltpu.VMEM((n, width, hidden), bf16),
            pltpu.VMEM((n, hidden, width), bf16),
            pltpu.VMEM(outgoing.shape, bf16),
            pltpu.VMEM((total * heads, HEAD_DIM), f32),
            pltpu.VMEM((n, height, width), bf16),
            pltpu.VMEM((height, hidden), f32),
            pltpu.VMEM((height, hidden), f32),
            pltpu.VMEM((height, hidden), bf16),
            pltpu.VMEM((n, half, width), f32),
            pltpu.VMEM((n, half, width), bf16),
            pltpu.VMEM((n, half, width), bf16),
            pltpu.VMEM((n, 4, total, width), bf16),
            pltpu.VMEM((n, total, width), bf16),
            pltpu.VMEM((n, 3, total, width), bf16),
            pltpu.VMEM((n, 2, total, width), bf16),
            pltpu.VMEM((n, 2, total, width), bf16),
            pltpu.VMEM((n, total, width), bf16),
            pltpu.VMEM((n, total, width), bf16),
            pltpu.VMEM(outgoing.shape, bf16),
            pltpu.VMEM(outgoing.shape, bf16),
            dma((3, n)),
            dma((2,)),
            dma((PARTS, 8)),
            dma((PARTS, 8)),
            dma((n, 8)),
            dma((n, 8)),
            dma((n, 8)),
            dma((n, 8)),
            dma((PARTS, 8)),
            dma((PARTS, 8)),
        ],
        compiler_params=pltpu.CompilerParams(
            collective_id=0, has_side_effects=True, vmem_limit_bytes=50 * 1024 * 1024
        ),
        name="experts",
    )(outgoing, gate_w, up_w, down_w)


def local(
    query,
    k_cache,
    v_cache,
    new_key,
    new_value,
    lengths,
    residual,
    norm_gain,
    router,
    routes,
    w_gate,
    w_up,
    w_down,
):
    rows = query.shape[0]
    width = query.shape[1]
    experts = lax.axis_size("grp")
    most = max(2, 2 * rows // experts)
    attended = attend(query, k_cache, v_cache, new_key, new_value, lengths)
    mixed = residual.astype(jnp.float32) + attended
    power = jnp.mean(mixed * mixed, axis=1, keepdims=True)
    normed = (mixed * lax.rsqrt(power + 1e-05) * norm_gain.astype(jnp.float32)).astype(jnp.bfloat16)
    logits = jnp.dot(normed, router, preferred_element_type=jnp.float32)
    chosen = routes[:, :, None] == jnp.arange(experts)[None, None, :]
    picked = jnp.sum(jnp.where(chosen, logits[:, None, :], 0.0), axis=-1)
    first = jax.nn.sigmoid(picked[:, 0] - picked[:, 1])
    second = jax.nn.sigmoid(picked[:, 1] - picked[:, 0])
    weights = jnp.stack([first, second], axis=1)
    ranks = slot_ranks(routes)
    slot_of = routes * most + ranks
    slot_range = jnp.arange(experts * most)
    placing = slot_of[:, :, None] == slot_range[None, None, :]
    one_hot = jnp.sum(placing.astype(jnp.float32), axis=1).astype(jnp.bfloat16)
    outgoing = jnp.einsum("rj,rx->jx", one_hot, normed, preferred_element_type=jnp.float32).astype(
        jnp.bfloat16
    )
    returned = run_experts(
        outgoing.reshape(experts * most, Q_HEADS, HEAD_DIM), w_gate[0], w_up[0], w_down[0]
    )
    returned = returned.reshape(experts * most, width).astype(jnp.float32)
    mixing = jnp.sum(jnp.where(placing, weights[:, :, None], 0.0), axis=1)
    combined = jnp.dot(
        mixing, returned, precision=lax.Precision.HIGHEST, preferred_element_type=jnp.float32
    )
    return (mixed + combined).astype(jnp.bfloat16)


def solution(mesh):
    placed = (
        P(("side", "grp", "cuts"), None),
        P(("side", "grp", "cuts"), None, None),
        P(("side", "grp", "cuts"), None, None),
        P(("side", "grp", "cuts"), None),
        P(("side", "grp", "cuts"), None),
        P(("side", "grp", "cuts")),
        P(("side", "grp", "cuts"), None),
        P(),
        P(),
        P(("side", "grp", "cuts"), None),
        P("grp", None, ("side", "cuts")),
        P("grp", None, ("side", "cuts")),
        P("grp", ("side", "cuts"), None),
    )
    return jax.shard_map(
        local,
        mesh=mesh,
        in_specs=placed,
        out_specs=P(("side", "grp", "cuts"), None),
        check_vma=False,
    )
```
